128 devices in a mesh: mgroup: 16 (over y_hi, z, core), msub: 8 (over x, y_lo).
Axes of the slice: x: 4, y: 4 (y_hi: 2, y_lo: 2; y = y_hi * 2 + y_lo), z: 4, core: 2. Of those that a mesh axis runs over, the one named last changes fastest.
Arguments:
- in_modes: int32 [128, 2], P(('mgroup', 'msub')), may hold values from 0 to 31
- back_first: bfloat16 [128, 1024, 2048], P(('mgroup', 'msub')), may hold values from -192 to 192
- back_second: bfloat16 [128, 1024, 2048], P(('mgroup', 'msub')), may hold values from -512 to 512
Outputs:
- mask_first: float32 [1024, 2048], P(('mgroup', 'msub'))
- mask_second: float32 [1024, 2048], P(('mgroup', 'msub'))
The draws below stay inside these ranges and needn't reach their ends.
Inputs may be any that keep to these rules, and one draw needn't show every extreme that they name: `in_modes`: each row holds a mode's row order and column order.
All inputs are finite; a program needn't handle non-finite values.
Results may differ from the reference program's by a relative error of at most 0.013.
Values may be sent and summed in bfloat16 or wider, within the bound.
No kernel may reach another device: no remote copies, remote signals or barrier semaphores. Data moves between devices by JAX's collectives and lax.ppermute only.
A program may use at most 128 MiB of HBM per device.

```python
import math
import jax
import jax.numpy as jnp
from jax import lax

G = 1024
ORDERS = 32
MODES = 128


def set_ends(result, own_key, least, largest):
    longest = result.shape.index(max(result.shape))
    spots = []
    for shift in (0, 1):
        where = [jax.random.randint(jax.random.fold_in(own_key, axis), (), 0, length) for axis, length in enumerate(result.shape)]
        where[longest] = (where[longest] + shift) % result.shape[longest]
        spots.append(tuple(where))
    return result.at[spots[0]].set(least).at[spots[1]].set(largest)


def strengthened(drawn, key, source, target, shards_of, factor):
    def block_of(axis_at):
        return (jnp.arange(drawn.shape[axis_at]) // (drawn.shape[axis_at] // shards_of)).reshape((-1,) + (1,) * (drawn.ndim - 1 - axis_at))

    one_side = jax.random.permutation(key, shards_of)[block_of(target)]
    second = (block_of(target) + shards_of // 2) % shards_of
    return jnp.where((block_of(source) == one_side) | (block_of(source) == second), factor * drawn, drawn)


def block_scale(key, dims, pieces, low, largest):
    level = 1.0
    for dim, blocks in pieces:
        heights = jax.random.uniform(jax.random.fold_in(jax.random.fold_in(key, 6), dim), (blocks,), jnp.float32, low / len(pieces), largest / len(pieces))
        level = level * jnp.repeat(jnp.exp(heights), dims[dim] // blocks).reshape((-1,) + (1,) * (len(dims) - 1 - dim))
    return level


def heavy_noise(own_key, shape, scale, reach, shards, heavy, kind=jnp.bfloat16):
    array = scale * jax.random.normal(own_key, shape, jnp.float32)
    if shards:
        array = array * block_scale(own_key, shape, shards, -0.22, 0.18)
    return jnp.clip(strengthened(array, jax.random.fold_in(own_key, 3), *heavy), -reach, reach).astype(kind)


def setup_inputs(seed: int = 0) -> dict:
    key_list = jax.random.split(jax.random.key(seed), 4)
    in_modes = set_ends(jax.random.randint(key_list[0], (MODES, 2), 0, ORDERS), jax.random.fold_in(key_list[0], 1), 0, ORDERS - 1).astype(jnp.int32)
    back_first = heavy_noise(key_list[1], (MODES, G, 2 * G), 8.0, 192.0, ((0, 128),), (0, 1, 128, 5.5))
    back_second = heavy_noise(key_list[2], (MODES, G, 2 * G), 24.0, 512.0, ((0, 128),), (0, 1, 128, 5.5))
    return dict(in_modes=in_modes, back_first=back_first, back_second=back_second)


span_width = 24.0

def grid_points(cells):
    index = jnp.arange(cells, dtype=jnp.float32)
    return (index - cells / 2 + 0.5) * (span_width / cells)

def hermite_table(points):
    before = jnp.zeros_like(points)
    current = math.pi ** (-0.25) * jnp.exp(-0.5 * points * points)
    collected = []
    for order in range(ORDERS):
        collected.append(current)
        following = math.sqrt(2.0 / (order + 1)) * points * current - math.sqrt(order / (order + 1.0)) * before
        before, current = (current, following)
    return jnp.stack(collected, axis=0)

def chirp_parts(cells):
    index = jnp.arange(cells, dtype=jnp.int32)
    offset = index[:, None] - index[None, :]
    square = offset * offset % (2 * cells)
    phase = square.astype(jnp.float32) * (math.pi / cells)
    factor = cells ** (-0.5)
    return ((jnp.cos(phase) * factor).astype(jnp.bfloat16), (jnp.sin(phase) * factor).astype(jnp.bfloat16))

def soften(intersection):
    half = intersection.shape[-1] // 2
    real_part = intersection[..., :half]
    imag_part = intersection[..., half:]
    denom = jnp.sqrt(real_part * real_part + imag_part * imag_part + 1.0)
    return intersection / jnp.concatenate([denom, denom], axis=-1)

def reference(in_modes, back_first, back_second):
    cells = G
    herm_table = hermite_table(grid_points(cells))
    row_funcs = herm_table[in_modes[:, 0]]
    col_funcs = herm_table[in_modes[:, 1]]
    chirp_real, chirp_imag = chirp_parts(cells)
    big_chirp = jnp.concatenate([jnp.concatenate([chirp_real, chirp_imag], axis=1), jnp.concatenate([-chirp_imag, chirp_real], axis=1)], axis=0)
    scale_all = float(MODES) ** (-0.5)

    def first_term(running, mode_item):
        row_one, col_one, back_one = mode_item
        fields = (row_one[:, None] * col_one[None, :]).astype(jnp.bfloat16).astype(jnp.float32)
        tiled = jnp.concatenate([fields, fields], axis=1)
        return (running + back_one.astype(jnp.float32) * tiled, None)
    intersection_one, _ = lax.scan(first_term, jnp.zeros((cells, 2 * cells), jnp.float32), (row_funcs, col_funcs, back_first))
    mask_first = soften(intersection_one * scale_all)
    mask_low = mask_first.astype(jnp.bfloat16).astype(jnp.float32)

    def second_term(running, mode_item):
        row_one, col_one, back_one = mode_item
        fields = (row_one[:, None] * col_one[None, :]).astype(jnp.bfloat16).astype(jnp.float32)
        tiled = jnp.concatenate([fields, fields], axis=1)
        applied = (mask_low * tiled).astype(jnp.bfloat16)
        spread = jnp.dot(applied, big_chirp, preferred_element_type=jnp.float32).astype(jnp.bfloat16)
        rotated = jnp.concatenate([-spread[:, cells:], spread[:, :cells]], axis=1)
        arrived = jnp.dot(chirp_real, spread, preferred_element_type=jnp.float32) + jnp.dot(chirp_imag, rotated, preferred_element_type=jnp.float32)
        back_full = back_one.astype(jnp.float32)
        back_real = back_full[:, :cells]
        back_imag = back_full[:, cells:]
        arr_real = arrived[:, :cells]
        arr_imag = arrived[:, cells:]
        term = jnp.concatenate([back_real * arr_real + back_imag * arr_imag, back_imag * arr_real - back_real * arr_imag], axis=1)
        return (running + term, None)
    intersection_two, _ = lax.scan(second_term, jnp.zeros((cells, 2 * cells), jnp.float32), (row_funcs, col_funcs, back_second))
    mask_second = soften(intersection_two * scale_all)
    return (mask_first, mask_second)
```

```python
import math

import jax
import jax.numpy as jnp
import numpy as np
from jax import lax
from jax.sharding import Mesh
from jax.sharding import PartitionSpec as P

ORDERS = 32
SPAN = 24.0
AXES = ("yh", "z", "core", "x", "yl")
PEERS = ("yh", "z", "x", "yl")
BF16 = jnp.bfloat16
F32 = jnp.float32


def hermite_table(cells):
    index = np.arange(cells, dtype=np.float32)
    points = ((index - np.float32(cells / 2) + np.float32(0.5)) * np.float32(SPAN / cells)).astype(np.float32)
    before = np.zeros_like(points)
    current = (np.float32(math.pi ** (-0.25)) * np.exp(np.float32(-0.5) * points * points)).astype(np.float32)
    collected = []
    for order in range(ORDERS):
        collected.append(current)
        following = (
            np.float32(math.sqrt(2.0 / (order + 1))) * points * current
            - np.float32(math.sqrt(order / (order + 1.0))) * before
        ).astype(np.float32)
        before, current = (current, following)
    return np.stack(collected, axis=0)


def chirp_halves(cells):
    half = cells // 2
    index = np.arange(half, dtype=np.int64)
    offset = index[:, None] - index[None, :]
    square = offset * offset % (2 * cells)
    phase = square.astype(np.float64) * (math.pi / cells)
    factor = cells ** (-0.5)
    real = (np.cos(phase) * factor).astype(np.float32)
    imag = (np.sin(phase) * factor).astype(np.float32)
    even = offset % 2 == 0
    out = []
    for keep in (even, ~even):
        r = np.where(keep, real, 0.0)
        i = np.where(keep, imag, 0.0)
        out.append((r.astype(jnp.bfloat16), i.astype(jnp.bfloat16)))
    return out


def soften(intersection):
    half = intersection.shape[-1] // 2
    real_part = intersection[..., :half]
    imag_part = intersection[..., half:]
    denom = jnp.sqrt(real_part * real_part + imag_part * imag_part + 1.0)
    return intersection / jnp.concatenate([denom, denom], axis=-1)


def swap_cores(block):
    return lax.ppermute(block, "core", [(0, 1), (1, 0)])


def reduce_rows(product):
    rows, width = product.shape
    core = lax.axis_index("core")
    split = product.reshape(8, 2, 64, width)
    away = lax.dynamic_index_in_dim(split, 1 - core, 1, keepdims=False).astype(BF16)
    keep = lax.dynamic_index_in_dim(split, core, 1, keepdims=False)
    both = (keep.astype(F32) + swap_cores(away).astype(F32)).astype(BF16)
    both = both.reshape(64, rows // 128, width)
    parts = lax.all_to_all(both, PEERS, 0, 0, tiled=True)
    return jnp.sum(parts.astype(F32), axis=0)


def gather_rows(own):
    rows, width = own.shape
    core = lax.axis_index("core")
    mine = lax.all_to_all(jnp.broadcast_to(own[None], (64, rows, width)), PEERS, 0, 0, tiled=True)
    mine = mine.reshape(8, 64, width)
    other = swap_cores(mine)
    first = jnp.where(core == 0, mine, other)
    second = jnp.where(core == 0, other, mine)
    return jnp.stack([first, second], axis=1).reshape(rows * 128, width)


def body(in_modes, back_first, back_second):
    cells = back_first.shape[1]
    half = cells // 2
    scale_all = float(128) ** (-0.5)
    table = jnp.asarray(hermite_table(cells))
    row_func = lax.dynamic_index_in_dim(table, in_modes[0, 0], 0, keepdims=False)
    col_func = lax.dynamic_index_in_dim(table, in_modes[0, 1], 0, keepdims=False)
    field = (row_func[:, None] * col_func[None, :]).astype(BF16).astype(F32)
    tiled = jnp.concatenate([field, field], axis=1)
    summed = reduce_rows(back_first[0].astype(F32) * tiled)
    mask_first = soften(summed * scale_all)
    mask_low = gather_rows(mask_first.astype(BF16))
    (even_r, even_i), (odd_r, odd_i) = jax.tree.map(jnp.asarray, chirp_halves(cells))
    right = []
    left = []
    for r, i in ((even_r, even_i), (odd_r, odd_i)):
        right.append(jnp.block([[r, i], [-i, r]]))
        left.append(jnp.block([[r, -i], [i, r]]))
    applied = (mask_low.astype(F32) * tiled).astype(BF16).astype(F32)
    real, imag = applied[:, :cells], applied[:, cells:]
    plus = jnp.concatenate([real[:, :half] + real[:, half:], imag[:, :half] + imag[:, half:]], axis=1).astype(BF16)
    minus = jnp.concatenate([real[:, :half] - real[:, half:], imag[:, :half] - imag[:, half:]], axis=1).astype(BF16)
    even = jnp.dot(plus, right[0], preferred_element_type=F32)
    odd = jnp.dot(minus, right[1], preferred_element_type=F32)
    low = (even + odd).astype(BF16).astype(F32)
    high = (even - odd).astype(BF16).astype(F32)

    def fold(part, sign):
        top, bottom = part[:half], part[half:]
        both = (top + sign * bottom).astype(BF16)
        return jnp.concatenate([both[:, :half], both[:, half:]], axis=0)

    sums = jnp.concatenate([fold(low, 1.0), fold(high, 1.0)], axis=1)
    diffs = jnp.concatenate([fold(low, -1.0), fold(high, -1.0)], axis=1)
    even = jnp.dot(left[0], sums, preferred_element_type=F32)
    odd = jnp.dot(left[1], diffs, preferred_element_type=F32)
    top = even + odd
    bottom = even - odd
    arr_real = jnp.concatenate([top[:half], bottom[:half]], axis=0)
    arr_imag = jnp.concatenate([top[half:], bottom[half:]], axis=0)
    back = back_second[0].astype(F32)
    back_real, back_imag = back[:, :cells], back[:, cells:]
    product = jnp.concatenate(
        [back_real * arr_real + back_imag * arr_imag, back_imag * arr_real - back_real * arr_imag], axis=1
    )
    mask_second = soften(reduce_rows(product) * scale_all)
    return (mask_first, mask_second)


def solution(mesh):
    fine = Mesh(mesh.devices.reshape(2, 4, 2, 4, 2), AXES)
    placed = (P(AXES, None), P(AXES, None, None), P(AXES, None, None))
    return jax.shard_map(
        body, mesh=fine, in_specs=placed, out_specs=(P(AXES, None), P(AXES, None)), check_vma=False
    )
```

```python
import functools
import math

import jax
import jax.numpy as jnp
import numpy as np
from jax import lax
from jax.experimental import pallas as pl
from jax.experimental.pallas import tpu as pltpu
from jax.sharding import Mesh
from jax.sharding import PartitionSpec as P

ORDERS = 32
SPAN = 24.0
AXES = ("yh", "z", "core", "x", "yl")
PEERS = ("yh", "z", "x", "yl")
BF16 = jnp.bfloat16
F32 = jnp.float32
ANY = pl.BlockSpec(memory_space=pl.ANY)
VMEM = pl.BlockSpec(memory_space=pltpu.VMEM)
SMEM = pl.BlockSpec(memory_space=pltpu.SMEM)
DMA = pltpu.SemaphoreType.DMA
PARAMS = pltpu.CompilerParams(vmem_limit_bytes=60000 * 1024)


def hermite_table(cells):
    index = np.arange(cells, dtype=np.float32)
    points = ((index - np.float32(cells / 2) + np.float32(0.5)) * np.float32(SPAN / cells)).astype(np.float32)
    before = np.zeros_like(points)
    current = (np.float32(math.pi ** (-0.25)) * np.exp(np.float32(-0.5) * points * points)).astype(np.float32)
    collected = []
    for order in range(ORDERS):
        collected.append(current)
        following = (
            np.float32(math.sqrt(2.0 / (order + 1))) * points * current
            - np.float32(math.sqrt(order / (order + 1.0))) * before
        ).astype(np.float32)
        before, current = (current, following)
    return np.stack(collected, axis=0)


def chirp_halves(cells):
    half = cells // 2
    index = np.arange(half, dtype=np.int64)
    offset = index[:, None] - index[None, :]
    square = offset * offset % (2 * cells)
    phase = square.astype(np.float64) * (math.pi / cells)
    factor = cells ** (-0.5)
    real = (np.cos(phase) * factor).astype(np.float32)
    imag = (np.sin(phase) * factor).astype(np.float32)
    even = offset % 2 == 0
    out = []
    for keep in (even, ~even):
        r = np.where(keep, real, 0.0)
        i = np.where(keep, imag, 0.0)
        out.append((r.astype(jnp.bfloat16), i.astype(jnp.bfloat16)))
    return out


def soften(intersection):
    half = intersection.shape[-1] // 2
    real_part = intersection[..., :half]
    imag_part = intersection[..., half:]
    denom = jnp.sqrt(real_part * real_part + imag_part * imag_part + 1.0)
    return intersection / jnp.concatenate([denom, denom], axis=-1)


def swap_cores(block):
    return lax.ppermute(block, "core", [(0, 1), (1, 0)])


def field_of(modes, table, columns, core):
    picked = columns[:, :, core].reshape(512, ORDERS)
    lanes = lax.broadcasted_iota(jnp.int32, picked.shape, 1)
    row_func = jnp.sum(jnp.where(lanes == modes[0, 0], picked, 0.0), axis=1, keepdims=True)
    col_func = table[pl.ds(modes[0, 1], 1), :]
    return (row_func * col_func).astype(BF16)


def first_kernel(away, modes, table, columns, *refs):
    if away:
        back, out, buf, sem = refs
        got = None
    else:
        got, back, out, buf, sem = refs
    core = lax.axis_index("core")
    if away:
        core = 1 - core
    copies = [pltpu.make_async_copy(back.at[h, :, core], buf.at[h], sem.at[h]) for h in range(2)]
    for copy in copies:
        copy.start()
    field = field_of(modes, table, columns, core)
    cells = field.shape[1]
    for h in range(2):
        copies[h].wait()
        part = field[h * 256 : (h + 1) * 256]
        for plane in range(2):
            span = slice(plane * cells, (plane + 1) * cells)
            block = buf[h, :, :, span].reshape(256, cells)
            if away:
                value = block * part
            else:
                value = block.astype(F32) * part.astype(F32)
                value = (value + got[h, :, :, span].reshape(256, cells).astype(F32)).astype(BF16)
            out[h, :, :, span] = value.reshape(4, 64, cells)


def first_product(modes, table, columns, back, got=None):
    width = back.shape[-1]
    away = got is None
    return pl.pallas_call(
        functools.partial(first_kernel, away),
        out_shape=jax.ShapeDtypeStruct((2, 4, 64, width), BF16),
        in_specs=[SMEM, VMEM, VMEM] + ([] if away else [VMEM]) + [ANY],
        out_specs=VMEM,
        scratch_shapes=[pltpu.VMEM((2, 4, 64, width), BF16), DMA((2,))],
        compiler_params=PARAMS,
        name="first_away" if away else "first_keep",
    )(modes, table, columns, *(() if away else (got,)), back)


def spread_half(mask, field, even, odd, sums, diffs, core):
    cells = field.shape[1]
    half = cells // 2
    real = mask[:, :, :, :cells].reshape(512, cells) * field
    imag = mask[:, :, :, cells:].reshape(512, cells) * (-field)
    plus = jnp.concatenate([real[:, :half] + real[:, half:], imag[:, :half] + imag[:, half:]], axis=1)
    minus = jnp.concatenate([real[:, :half] - real[:, half:], imag[:, :half] - imag[:, half:]], axis=1)
    for n in range(4):
        span = slice(n * 256, (n + 1) * 256)
        e = jnp.dot(plus, even[:, :, :, :, span].reshape(cells, 256), preferred_element_type=F32)
        o = jnp.dot(minus, odd[:, :, :, :, span].reshape(cells, 256), preferred_element_type=F32)
        plane, at = n // 2, (n % 2) * 256
        for shift, value in ((0, e + o), (half, e - o)):
            value = (-value if plane else value).astype(BF16)
            top, bottom = value[:256], value[256:]
            where = slice(at + shift, at + shift + 256)
            sums[plane, :, core, :, where] = (top + bottom).reshape(4, 64, 256)
            diffs[plane, :, core, :, where] = (top - bottom).reshape(4, 64, 256)


def second_half(even, odd, sums, diffs, back, out, core):
    cells = sums.shape[-1]
    rows_even = even[:, :, core].reshape(512, cells)
    rows_odd = odd[:, :, core].reshape(512, cells)
    for n in range(4):
        span = slice(n * 256, (n + 1) * 256)
        e = jnp.dot(rows_even, sums[:, :, :, :, span].reshape(cells, 256), preferred_element_type=F32)
        o = jnp.dot(rows_odd, diffs[:, :, :, :, span].reshape(cells, 256), preferred_element_type=F32)
        other = slice(cells + n * 256, cells + (n + 1) * 256)
        for h, value in ((0, e + o), (1, e - o)):
            real, imag = value[:256], value[256:]
            back_real = back[h, :, :, span].reshape(256, 256).astype(F32)
            back_imag = back[h, :, :, other].reshape(256, 256).astype(F32)
            out[h, :, :, span] = (back_real * real + back_imag * imag).astype(BF16).reshape(4, 64, 256)
            out[h, :, :, other] = (back_imag * real - back_real * imag).astype(BF16).reshape(4, 64, 256)


def spread_kernel(modes, table, columns, mask, even, odd, sums, diffs):
    core = lax.axis_index("core")
    field = field_of(modes, table, columns, core)
    spread_half(mask, field, even, odd, sums, diffs, 0)


def spread_own(modes, table, columns, mask, even, odd):
    cells = even.shape[-1]
    shape = jax.ShapeDtypeStruct((2, 4, 1, 64, cells), BF16)
    return pl.pallas_call(
        spread_kernel,
        out_shape=(shape, shape),
        in_specs=[SMEM] + [VMEM] * 5,
        out_specs=(VMEM, VMEM),
        compiler_params=PARAMS,
        name="spread_own",
    )(modes, table, columns, mask, even, odd)


def arrive_kernel(modes, table, columns, mask, even, odd, own_sums, own_diffs, back, out, sums, diffs, buf, sem):
    core = lax.axis_index("core")
    other = 1 - core
    copy = pltpu.make_async_copy(back.at[:, :, other], buf, sem)
    copy.start()
    field = field_of(modes, table, columns, other)
    spread_half(mask, field, even, odd, sums, diffs, other)
    sums[:, :, core] = own_sums[:, :, 0]
    diffs[:, :, core] = own_diffs[:, :, 0]
    copy.wait()
    second_half(even, odd, sums, diffs, buf, out, other)


def arrive_away(modes, table, columns, mask, even, odd, own_sums, own_diffs, back):
    width = back.shape[-1]
    cells = width // 2
    shape = jax.ShapeDtypeStruct((2, 4, 2, 64, cells), BF16)
    return pl.pallas_call(
        arrive_kernel,
        out_shape=(jax.ShapeDtypeStruct((2, 4, 64, width), BF16), shape, shape),
        in_specs=[SMEM] + [VMEM] * 7 + [ANY],
        out_specs=(VMEM, VMEM, VMEM),
        scratch_shapes=[pltpu.VMEM((2, 4, 64, width), BF16), DMA],
        compiler_params=PARAMS,
        name="arrive_away",
    )(modes, table, columns, mask, even, odd, own_sums, own_diffs, back)


def keep_kernel(even, odd, sums, diffs, back, out, buf, sem):
    core = lax.axis_index("core")
    copy = pltpu.make_async_copy(back.at[:, :, core], buf, sem)
    copy.start()
    copy.wait()
    second_half(even, odd, sums, diffs, buf, out, core)


def arrive_keep(even, odd, sums, diffs, back):
    width = back.shape[-1]
    return pl.pallas_call(
        keep_kernel,
        out_shape=jax.ShapeDtypeStruct((2, 4, 64, width), BF16),
        in_specs=[VMEM] * 4 + [ANY],
        out_specs=VMEM,
        scratch_shapes=[pltpu.VMEM((2, 4, 64, width), BF16), DMA],
        compiler_params=PARAMS,
        name="arrive_keep",
    )(even, odd, sums, diffs, back)


def scatter_rows(both):
    width = both.shape[-1]
    parts = lax.all_to_all(both.reshape(64, 8, width), PEERS, 0, 0, tiled=True)
    return jnp.sum(parts.astype(F32), axis=0)


def body(modes, back_first, back_second):
    cells = back_first.shape[1]
    scale_all = float(128) ** (-0.5)
    host_table = hermite_table(cells)
    table = jnp.asarray(host_table)
    columns = jnp.asarray(host_table.T.copy()).reshape(2, 4, 2, 64, ORDERS)
    (even_r, even_i), (odd_r, odd_i) = jax.tree.map(jnp.asarray, chirp_halves(cells))
    even = jnp.block([[even_r, -even_i], [even_i, even_r]]).reshape(2, 4, 2, 64, cells)
    odd = jnp.block([[odd_r, -odd_i], [odd_i, odd_r]]).reshape(2, 4, 2, 64, cells)
    back_first = back_first.reshape(2, 4, 2, 64, 2 * cells)
    back_second = back_second.reshape(2, 4, 2, 64, 2 * cells)
    got = swap_cores(first_product(modes, table, columns, back_first))
    summed = scatter_rows(first_product(modes, table, columns, back_first, got))
    mask_first = soften(summed * scale_all)
    low = jnp.broadcast_to(mask_first.astype(BF16)[None], (64, 8, 2 * cells))
    mine = lax.all_to_all(low, PEERS, 0, 0, tiled=True).reshape(2, 4, 64, 2 * cells)
    other = swap_cores(mine)
    own = spread_own(modes, table, columns, mine, even, odd)
    away, sums, diffs = arrive_away(modes, table, columns, other, even, odd, *own, back_second)
    got = swap_cores(away)
    keep = arrive_keep(even, odd, sums, diffs, back_second)
    summed = scatter_rows((keep.astype(F32) + got.astype(F32)).astype(BF16))
    mask_second = soften(summed * scale_all)
    return (mask_first, mask_second)


def solution(mesh):
    fine = Mesh(mesh.devices.reshape(2, 4, 2, 4, 2), AXES)
    placed = (P(AXES, None), P(AXES, None, None), P(AXES, None, None))
    return jax.shard_map(
        body, mesh=fine, in_specs=placed, out_specs=(P(AXES, None), P(AXES, None)), check_vma=False
    )
```

```python
import functools
import math

import jax
import jax.numpy as jnp
import numpy as np
from jax import lax
from jax.experimental import pallas as pl
from jax.experimental.pallas import tpu as pltpu
from jax.sharding import Mesh
from jax.sharding import PartitionSpec as P

ORDERS = 32
SPAN = 24.0
AXES = ("yh", "z", "core", "x", "yl")
BF16 = jnp.bfloat16
F32 = jnp.float32
ANY = pl.BlockSpec(memory_space=pl.ANY)
VMEM = pl.BlockSpec(memory_space=pltpu.VMEM)
SMEM = pl.BlockSpec(memory_space=pltpu.SMEM)
DMA = pltpu.SemaphoreType.DMA


def params(mib):
    return pltpu.CompilerParams(vmem_limit_bytes=mib << 20)


def hermite_table(cells):
    index = np.arange(cells, dtype=np.float32)
    points = ((index - np.float32(cells / 2) + np.float32(0.5)) * np.float32(SPAN / cells)).astype(np.float32)
    before = np.zeros_like(points)
    current = (np.float32(math.pi ** (-0.25)) * np.exp(np.float32(-0.5) * points * points)).astype(np.float32)
    collected = []
    for order in range(ORDERS):
        collected.append(current)
        following = (
            np.float32(math.sqrt(2.0 / (order + 1))) * points * current
            - np.float32(math.sqrt(order / (order + 1.0))) * before
        ).astype(np.float32)
        before, current = (current, following)
    return np.stack(collected, axis=0)


def chirp_halves(cells):
    half = cells // 2
    index = np.arange(half, dtype=np.int64)
    offset = index[:, None] - index[None, :]
    square = offset * offset % (2 * cells)
    phase = square.astype(np.float64) * (math.pi / cells)
    factor = cells ** (-0.5)
    real = (np.cos(phase) * factor).astype(np.float32)
    imag = (np.sin(phase) * factor).astype(np.float32)
    even = offset % 2 == 0
    out = []
    for keep in (even, ~even):
        r = np.where(keep, real, 0.0)
        i = np.where(keep, imag, 0.0)
        out.append((r.astype(jnp.bfloat16), i.astype(jnp.bfloat16)))
    return out


def soften(intersection):
    half = intersection.shape[-1] // 2
    real_part = intersection[..., :half]
    imag_part = intersection[..., half:]
    denom = jnp.sqrt(real_part * real_part + imag_part * imag_part + 1.0)
    return intersection / jnp.concatenate([denom, denom], axis=-1)


def swap_cores(block):
    return lax.ppermute(block, "core", [(0, 1), (1, 0)])


def row_of(modes, columns, core):
    picked = columns[:, :, core].reshape(512, ORDERS)
    lanes = lax.broadcasted_iota(jnp.int32, picked.shape, 1)
    return jnp.sum(jnp.where(lanes == modes[0, 0], picked, 0.0), axis=1, keepdims=True)


def bits_of(spot):
    return (spot & 1) ^ (spot >> 1), spot >> 1


def owner_codes():
    out = []
    for yh in range(2):
        for z in range(4):
            for x in range(4):
                for yl in range(2):
                    (ax, bx), (ay, by), (az, bz) = bits_of(x), bits_of(yh * 2 + yl), bits_of(z)
                    out.append((ax * 4 + ay * 2 + az, bx * 4 + by * 2 + bz))
    return out


CODES = owner_codes()


def place_of(block, core):
    a, b = CODES[block]
    return a * 8 + b + core * (7 * b - 7 * a)


def device_groups():
    def device(a, b, core):
        x, y, z = ((a >> k & 1) ^ (3 * (b >> k & 1)) for k in (2, 1, 0))
        return ((((y >> 1) * 4 + z) * 2 + core) * 4 + x) * 2 + (y & 1)

    over_a = [[[device(a, b, core) for a in range(8)] for b in range(8)] for core in range(2)]
    over_b = [[[device(a, b, core) for b in range(8)] for a in range(8)] for core in range(2)]
    return over_a[0] + over_b[1], over_b[0] + over_a[1]


WIDE, NARROW = device_groups()


def first_kernel(away, modes, table, columns, *refs):
    if away:
        back, out, buf, sems = refs
        got = None
    else:
        got, back, out, buf, sems = refs
    core = lax.axis_index("core")
    if away:
        core = 1 - core
    copies = [
        pltpu.make_async_copy(back.at[k // 4, k % 4, core], buf.at[k], sems.at[k]) for k in range(8)
    ]
    for copy in copies:
        copy.start()
    row_func = row_of(modes, columns, core)
    col_func = table[pl.ds(modes[0, 1], 1), :]
    cells = col_func.shape[1]
    for k in range(8):
        copies[k].wait()
        for j in range(8):
            block = k * 8 + j
            place = place_of(block, core)
            field = (row_func[block * 8 : block * 8 + 8] * col_func).astype(BF16).astype(F32)
            for plane in range(2):
                span = slice(plane * cells, (plane + 1) * cells)
                value = buf[k, j * 8 : j * 8 + 8, span].astype(F32) * field
                if not away:
                    value = value + got[place, :, span].astype(F32)
                out[place, :, span] = value.astype(BF16)


def first_product(modes, table, columns, back, got=None):
    width = back.shape[-1]
    away = got is None
    return pl.pallas_call(
        functools.partial(first_kernel, away),
        out_shape=jax.ShapeDtypeStruct((64, 8, width), BF16),
        in_specs=[SMEM, VMEM, VMEM] + ([] if away else [VMEM]) + [ANY],
        out_specs=VMEM,
        scratch_shapes=[pltpu.VMEM((8, 64, width), BF16), DMA((8,))],
        compiler_params=params(14),
        name="first_away" if away else "first_keep",
    )(modes, table, columns, *(() if away else (got,)), back)


def spread_half(modes, table, columns, mask, even, odd, plus, minus, sums, diffs, core, slot):
    row_func = row_of(modes, columns, core)
    col_func = table[pl.ds(modes[0, 1], 1), :]
    cells = col_func.shape[1]
    half = cells // 2
    for pair in range(32):
        kept = []
        for block in (2 * pair, 2 * pair + 1):
            place = place_of(block, core)
            field = (row_func[block * 8 : block * 8 + 8] * col_func).astype(BF16).astype(F32)
            kept.append((mask[place, :, :cells].astype(F32) * field, mask[place, :, cells:].astype(F32) * (-field)))
        rows = slice(pair * 16, pair * 16 + 16)
        for plane in range(2):
            both = jnp.concatenate([kept[0][plane], kept[1][plane]], axis=0)
            span = slice(plane * half, (plane + 1) * half)
            plus[rows, span] = (both[:, :half] + both[:, half:]).astype(BF16)
            minus[rows, span] = (both[:, :half] - both[:, half:]).astype(BF16)
    for n in range(4):
        span = slice(n * 256, (n + 1) * 256)
        e = jnp.dot(plus[...], even[:, :, :, :, span].reshape(cells, 256), preferred_element_type=F32)
        o = jnp.dot(minus[...], odd[:, :, :, :, span].reshape(cells, 256), preferred_element_type=F32)
        plane, at = n // 2, (n % 2) * 256
        for shift, value in ((0, e + o), (half, e - o)):
            value = (-value if plane else value).astype(BF16)
            top, bottom = value[:256], value[256:]
            where = slice(at + shift, at + shift + 256)
            sums[plane, :, slot, :, where] = (top + bottom).reshape(4, 64, 256)
            diffs[plane, :, slot, :, where] = (top - bottom).reshape(4, 64, 256)


def second_half(even, odd, sums, diffs, back, out, core):
    cells = sums.shape[-1]
    rows_even = even[:, :, core].reshape(512, cells)
    rows_odd = odd[:, :, core].reshape(512, cells)
    for n in range(4):
        span = slice(n * 256, (n + 1) * 256)
        e = jnp.dot(rows_even, sums[:, :, :, :, span].reshape(cells, 256), preferred_element_type=F32)
        o = jnp.dot(rows_odd, diffs[:, :, :, :, span].reshape(cells, 256), preferred_element_type=F32)
        other = slice(cells + n * 256, cells + (n + 1) * 256)
        for h, value in ((0, e + o), (1, e - o)):
            real, imag = value[:256], value[256:]
            back_real = back[h, :, :, span].reshape(256, 256).astype(F32)
            back_imag = back[h, :, :, other].reshape(256, 256).astype(F32)
            new_real = back_real * real + back_imag * imag
            new_imag = back_imag * real - back_real * imag
            for j in range(32):
                place = place_of(h * 32 + j, core)
                out[place, :, span] = new_real[j * 8 : j * 8 + 8].astype(BF16)
                out[place, :, other] = new_imag[j * 8 : j * 8 + 8].astype(BF16)


def spread_kernel(modes, table, columns, mask, even, odd, sums, diffs, plus, minus):
    core = lax.axis_index("core")
    spread_half(modes, table, columns, mask, even, odd, plus, minus, sums, diffs, core, 0)


def spread_own(modes, table, columns, mask, even, odd):
    cells = even.shape[-1]
    shape = jax.ShapeDtypeStruct((2, 4, 1, 64, cells), BF16)
    return pl.pallas_call(
        spread_kernel,
        out_shape=(shape, shape),
        in_specs=[SMEM] + [VMEM] * 5,
        out_specs=(VMEM, VMEM),
        scratch_shapes=[pltpu.VMEM((512, cells), BF16)] * 2,
        compiler_params=params(20),
        name="spread_own",
    )(modes, table, columns, mask, even, odd)


def arrive_kernel(
    modes, table, columns, mask, even, odd, own_sums, own_diffs, back, out, sums, diffs, buf, plus, minus, sem
):
    core = lax.axis_index("core")
    other = 1 - core
    copy = pltpu.make_async_copy(back.at[:, :, other], buf, sem)
    copy.start()
    spread_half(modes, table, columns, mask, even, odd, plus, minus, sums, diffs, other, other)
    sums[:, :, core] = own_sums[:, :, 0]
    diffs[:, :, core] = own_diffs[:, :, 0]
    copy.wait()
    second_half(even, odd, sums, diffs, buf, out, other)


def arrive_away(modes, table, columns, mask, even, odd, own_sums, own_diffs, back):
    width = back.shape[-1]
    cells = width // 2
    shape = jax.ShapeDtypeStruct((2, 4, 2, 64, cells), BF16)
    return pl.pallas_call(
        arrive_kernel,
        out_shape=(jax.ShapeDtypeStruct((64, 8, width), BF16), shape, shape),
        in_specs=[SMEM] + [VMEM] * 7 + [ANY],
        out_specs=(VMEM, VMEM, VMEM),
        scratch_shapes=[pltpu.VMEM((2, 4, 64, width), BF16)] + [pltpu.VMEM((512, cells), BF16)] * 2 + [DMA],
        compiler_params=params(28),
        name="arrive_away",
    )(modes, table, columns, mask, even, odd, own_sums, own_diffs, back)


def keep_kernel(even, odd, sums, diffs, back, out, buf, sem):
    core = lax.axis_index("core")
    copy = pltpu.make_async_copy(back.at[:, :, core], buf, sem)
    copy.start()
    copy.wait()
    second_half(even, odd, sums, diffs, buf, out, core)


def arrive_keep(even, odd, sums, diffs, back):
    width = back.shape[-1]
    return pl.pallas_call(
        keep_kernel,
        out_shape=jax.ShapeDtypeStruct((64, 8, width), BF16),
        in_specs=[VMEM] * 4 + [ANY],
        out_specs=VMEM,
        scratch_shapes=[pltpu.VMEM((2, 4, 64, width), BF16), DMA],
        compiler_params=params(20),
        name="arrive_keep",
    )(even, odd, sums, diffs, back)


def exchange(blocks, groups):
    return lax.all_to_all(blocks, AXES, 0, 0, tiled=True, axis_index_groups=groups)


def total(parts):
    kept = [parts[k].astype(F32) for k in range(parts.shape[0])]
    while len(kept) > 1:
        kept = [kept[k] + kept[k + 1] for k in range(0, len(kept), 2)]
    return kept[0]


def scatter_rows(both):
    width = both.shape[-1]
    wide = exchange(both.reshape(8, 64, width), WIDE)
    partial = total(wide).astype(BF16)
    parts = exchange(partial.reshape(8, 8, width), NARROW)
    return total(parts)


def gather_rows(own):
    rows, width = own.shape
    near = exchange(jnp.broadcast_to(own[None], (8, rows, width)), NARROW)
    near = near.reshape(1, 8 * rows, width)
    wide = exchange(jnp.broadcast_to(near, (8, 8 * rows, width)), WIDE)
    return wide.reshape(64, rows, width)


def body(modes, back_first, back_second):
    cells = back_first.shape[1]
    scale_all = float(128) ** (-0.5)
    host_table = hermite_table(cells)
    table = jnp.asarray(host_table)
    columns = jnp.asarray(host_table.T.copy()).reshape(2, 4, 2, 64, ORDERS)
    (even_r, even_i), (odd_r, odd_i) = jax.tree.map(jnp.asarray, chirp_halves(cells))
    even = jnp.block([[even_r, -even_i], [even_i, even_r]]).reshape(2, 4, 2, 64, cells)
    odd = jnp.block([[odd_r, -odd_i], [odd_i, odd_r]]).reshape(2, 4, 2, 64, cells)
    back_first = back_first.reshape(2, 4, 2, 64, 2 * cells)
    back_second = back_second.reshape(2, 4, 2, 64, 2 * cells)
    got = swap_cores(first_product(modes, table, columns, back_first))
    summed = scatter_rows(first_product(modes, table, columns, back_first, got))
    mask_first = soften(summed * scale_all)
    mine = gather_rows(mask_first.astype(BF16))
    other = swap_cores(mine)
    own = spread_own(modes, table, columns, mine, even, odd)
    away, sums, diffs = arrive_away(modes, table, columns, other, even, odd, *own, back_second)
    got = swap_cores(away)
    keep = arrive_keep(even, odd, sums, diffs, back_second)
    summed = scatter_rows((keep.astype(F32) + got.astype(F32)).astype(BF16))
    mask_second = soften(summed * scale_all)
    return (mask_first, mask_second)


def solution(mesh):
    fine = Mesh(mesh.devices.reshape(2, 4, 2, 4, 2), AXES)
    placed = (P(AXES, None), P(AXES, None, None), P(AXES, None, None))
    return jax.shard_map(
        body, mesh=fine, in_specs=placed, out_specs=(P(AXES, None), P(AXES, None)), check_vma=False
    )
```

```python
import functools
import math

import jax
import jax.numpy as jnp
import numpy as np
from jax import lax
from jax.experimental import pallas as pl
from jax.experimental.pallas import tpu as pltpu
from jax.sharding import Mesh
from jax.sharding import PartitionSpec as P

ORDERS = 32
SPAN = 24.0
AXES = ("yh", "z", "core", "x", "yl")
BF16 = jnp.bfloat16
F32 = jnp.float32
ANY = pl.BlockSpec(memory_space=pl.ANY)
VMEM = pl.BlockSpec(memory_space=pltpu.VMEM)
SMEM = pl.BlockSpec(memory_space=pltpu.SMEM)
DMA = pltpu.SemaphoreType.DMA


def params(mib):
    return pltpu.CompilerParams(vmem_limit_bytes=mib << 20)


def hermite_table(cells):
    index = np.arange(cells, dtype=np.float32)
    points = ((index - np.float32(cells / 2) + np.float32(0.5)) * np.float32(SPAN / cells)).astype(np.float32)
    before = np.zeros_like(points)
    current = (np.float32(math.pi ** (-0.25)) * np.exp(np.float32(-0.5) * points * points)).astype(np.float32)
    collected = []
    for order in range(ORDERS):
        collected.append(current)
        following = (
            np.float32(math.sqrt(2.0 / (order + 1))) * points * current
            - np.float32(math.sqrt(order / (order + 1.0))) * before
        ).astype(np.float32)
        before, current = (current, following)
    return np.stack(collected, axis=0)


def chirp_halves(cells):
    half = cells // 2
    index = np.arange(half, dtype=np.int64)
    offset = index[:, None] - index[None, :]
    square = offset * offset % (2 * cells)
    phase = square.astype(np.float64) * (math.pi / cells)
    factor = cells ** (-0.5)
    real = (np.cos(phase) * factor).astype(np.float32)
    imag = (np.sin(phase) * factor).astype(np.float32)
    even = offset % 2 == 0
    out = []
    for keep in (even, ~even):
        r = np.where(keep, real, 0.0)
        i = np.where(keep, imag, 0.0)
        out.append((r.astype(jnp.bfloat16), i.astype(jnp.bfloat16)))
    return out


def soften(intersection):
    half = intersection.shape[-1] // 2
    real_part = intersection[..., :half]
    imag_part = intersection[..., half:]
    denom = jnp.sqrt(real_part * real_part + imag_part * imag_part + 1.0)
    return intersection / jnp.concatenate([denom, denom], axis=-1)


def swap_cores(block):
    return lax.ppermute(block, "core", [(0, 1), (1, 0)])


def row_of(modes, columns, core):
    picked = columns[:, :, core].reshape(512, ORDERS)
    lanes = lax.broadcasted_iota(jnp.int32, picked.shape, 1)
    return jnp.sum(jnp.where(lanes == modes[0, 0], picked, 0.0), axis=1, keepdims=True)


def bits_of(spot):
    return (spot & 1) ^ (spot >> 1), spot >> 1


def owner_codes():
    out = []
    for yh in range(2):
        for z in range(4):
            for x in range(4):
                for yl in range(2):
                    (ax, bx), (ay, by), (az, bz) = bits_of(x), bits_of(yh * 2 + yl), bits_of(z)
                    out.append((ax * 4 + ay * 2 + az, bx * 4 + by * 2 + bz))
    return out


CODES = owner_codes()


def place_of(block, core):
    a, b = CODES[block]
    return a * 8 + b + core * (7 * b - 7 * a)


def device_groups():
    def device(a, b, core):
        x, y, z = ((a >> k & 1) ^ (3 * (b >> k & 1)) for k in (2, 1, 0))
        return ((((y >> 1) * 4 + z) * 2 + core) * 4 + x) * 2 + (y & 1)

    over_a = [[[device(a, b, core) for a in range(8)] for b in range(8)] for core in range(2)]
    over_b = [[[device(a, b, core) for b in range(8)] for a in range(8)] for core in range(2)]
    return over_a[0] + over_b[1], over_b[0] + over_a[1]


WIDE, NARROW = device_groups()


def first_kernel(away, modes, table, columns, back, out, buf, sems):
    core = lax.axis_index("core")
    if away:
        core = 1 - core
    copies = [
        pltpu.make_async_copy(back.at[k // 4, k % 4, core], buf.at[k], sems.at[k]) for k in range(8)
    ]
    for copy in copies:
        copy.start()
    row_func = row_of(modes, columns, core)
    col_func = table[pl.ds(modes[0, 1], 1), :]
    cells = col_func.shape[1]
    for k in range(8):
        copies[k].wait()
        for j in range(8):
            block = k * 8 + j
            place = place_of(block, core)
            field = (row_func[block * 8 : block * 8 + 8] * col_func).astype(BF16).astype(F32)
            for plane in range(2):
                span = slice(plane * cells, (plane + 1) * cells)
                out[place, :, span] = (buf[k, j * 8 : j * 8 + 8, span].astype(F32) * field).astype(BF16)


def first_product(modes, table, columns, back, away):
    width = back.shape[-1]
    return pl.pallas_call(
        functools.partial(first_kernel, away),
        out_shape=jax.ShapeDtypeStruct((64, 8, width), BF16),
        in_specs=[SMEM, VMEM, VMEM, ANY],
        out_specs=VMEM,
        scratch_shapes=[pltpu.VMEM((8, 64, width), BF16), DMA((8,))],
        compiler_params=params(60 if away else 14),
        cost_estimate=pl.CostEstimate(flops=2 << 20, bytes_accessed=4 << 20, transcendentals=0),
        name="first_away" if away else "first_keep",
    )(modes, table, columns, back)


def spread_half(modes, table, columns, mask, even, odd, plus, minus, sums, diffs, core, slot):
    row_func = row_of(modes, columns, core)
    col_func = table[pl.ds(modes[0, 1], 1), :]
    cells = col_func.shape[1]
    half = cells // 2
    for pair in range(32):
        kept = []
        for block in (2 * pair, 2 * pair + 1):
            place = place_of(block, core)
            field = (row_func[block * 8 : block * 8 + 8] * col_func).astype(BF16).astype(F32)
            kept.append((mask[place, :, :cells].astype(F32) * field, mask[place, :, cells:].astype(F32) * (-field)))
        rows = slice(pair * 16, pair * 16 + 16)
        for plane in range(2):
            both = jnp.concatenate([kept[0][plane], kept[1][plane]], axis=0)
            span = slice(plane * half, (plane + 1) * half)
            plus[rows, span] = (both[:, :half] + both[:, half:]).astype(BF16)
            minus[rows, span] = (both[:, :half] - both[:, half:]).astype(BF16)
    for n in range(4):
        span = slice(n * 256, (n + 1) * 256)
        e = jnp.dot(plus[...], even[:, :, :, :, span].reshape(cells, 256), preferred_element_type=F32)
        o = jnp.dot(minus[...], odd[:, :, :, :, span].reshape(cells, 256), preferred_element_type=F32)
        plane, at = n // 2, (n % 2) * 256
        for shift, value in ((0, e + o), (half, e - o)):
            value = (-value if plane else value).astype(BF16)
            top, bottom = value[:256], value[256:]
            where = slice(at + shift, at + shift + 256)
            sums[plane, :, slot, :, where] = (top + bottom).reshape(4, 64, 256)
            diffs[plane, :, slot, :, where] = (top - bottom).reshape(4, 64, 256)


def second_half(even, odd, sums, diffs, back, out, core):
    cells = sums.shape[-1]
    rows_even = even[:, :, core].reshape(512, cells)
    rows_odd = odd[:, :, core].reshape(512, cells)
    for n in range(4):
        span = slice(n * 256, (n + 1) * 256)
        e = jnp.dot(rows_even, sums[:, :, :, :, span].reshape(cells, 256), preferred_element_type=F32)
        o = jnp.dot(rows_odd, diffs[:, :, :, :, span].reshape(cells, 256), preferred_element_type=F32)
        other = slice(cells + n * 256, cells + (n + 1) * 256)
        for h, value in ((0, e + o), (1, e - o)):
            real, imag = value[:256], value[256:]
            back_real = back[h, :, :, span].reshape(256, 256).astype(F32)
            back_imag = back[h, :, :, other].reshape(256, 256).astype(F32)
            new_real = back_real * real + back_imag * imag
            new_imag = back_imag * real - back_real * imag
            for j in range(32):
                place = place_of(h * 32 + j, core)
                out[place, :, span] = new_real[j * 8 : j * 8 + 8].astype(BF16)
                out[place, :, other] = new_imag[j * 8 : j * 8 + 8].astype(BF16)


def spread_kernel(modes, table, columns, mask, even, odd, sums, diffs, plus, minus):
    core = lax.axis_index("core")
    spread_half(modes, table, columns, mask, even, odd, plus, minus, sums, diffs, core, 0)


def spread_own(modes, table, columns, mask, even, odd):
    cells = even.shape[-1]
    shape = jax.ShapeDtypeStruct((2, 4, 1, 64, cells), BF16)
    return pl.pallas_call(
        spread_kernel,
        out_shape=(shape, shape),
        in_specs=[SMEM] + [VMEM] * 5,
        out_specs=(VMEM, VMEM),
        scratch_shapes=[pltpu.VMEM((512, cells), BF16)] * 2,
        compiler_params=params(20),
        name="spread_own",
    )(modes, table, columns, mask, even, odd)


def arrive_kernel(
    modes, table, columns, mask, even, odd, own_sums, own_diffs, back, out, sums, diffs, buf, plus, minus, sem
):
    core = lax.axis_index("core")
    other = 1 - core
    copy = pltpu.make_async_copy(back.at[:, :, other], buf, sem)
    copy.start()
    spread_half(modes, table, columns, mask, even, odd, plus, minus, sums, diffs, other, other)
    sums[:, :, core] = own_sums[:, :, 0]
    diffs[:, :, core] = own_diffs[:, :, 0]
    copy.wait()
    second_half(even, odd, sums, diffs, buf, out, other)


def arrive_away(modes, table, columns, mask, even, odd, own_sums, own_diffs, back):
    width = back.shape[-1]
    cells = width // 2
    shape = jax.ShapeDtypeStruct((2, 4, 2, 64, cells), BF16)
    return pl.pallas_call(
        arrive_kernel,
        out_shape=(jax.ShapeDtypeStruct((64, 8, width), BF16), shape, shape),
        in_specs=[SMEM] + [VMEM] * 7 + [ANY],
        out_specs=(VMEM, VMEM, VMEM),
        scratch_shapes=[pltpu.VMEM((2, 4, 64, width), BF16)] + [pltpu.VMEM((512, cells), BF16)] * 2 + [DMA],
        compiler_params=params(28),
        name="arrive_away",
    )(modes, table, columns, mask, even, odd, own_sums, own_diffs, back)


def keep_kernel(even, odd, sums, diffs, back, out, buf, sem):
    core = lax.axis_index("core")
    copy = pltpu.make_async_copy(back.at[:, :, core], buf, sem)
    copy.start()
    copy.wait()
    second_half(even, odd, sums, diffs, buf, out, core)


def arrive_keep(even, odd, sums, diffs, back):
    width = back.shape[-1]
    return pl.pallas_call(
        keep_kernel,
        out_shape=jax.ShapeDtypeStruct((64, 8, width), BF16),
        in_specs=[VMEM] * 4 + [ANY],
        out_specs=VMEM,
        scratch_shapes=[pltpu.VMEM((2, 4, 64, width), BF16), DMA],
        compiler_params=params(20),
        name="arrive_keep",
    )(even, odd, sums, diffs, back)


def exchange(blocks, groups):
    return lax.all_to_all(blocks, AXES, 0, 0, tiled=True, axis_index_groups=groups)


def total(parts):
    kept = [parts[k].astype(F32) for k in range(len(parts))]
    while len(kept) > 1:
        kept = [kept[k] + kept[k + 1] for k in range(0, len(kept), 2)]
    return kept[0]


def halve_rows(both):
    width = both.shape[-1]
    return total(exchange(both.reshape(8, 64, width), WIDE)).astype(BF16)


def own_place():
    pairs = [bits_of(lax.axis_index("x")), bits_of(lax.axis_index("yh") * 2 + lax.axis_index("yl"))]
    pairs.append(bits_of(lax.axis_index("z")))
    a, b = (pairs[0][k] * 4 + pairs[1][k] * 2 + pairs[2][k] for k in range(2))
    return b + lax.axis_index("core") * (a - b)


def mask_kernel(scale, near, low, own, every):
    cells = near.shape[-1] // 2
    for block in range(8):
        rows = slice(block * 8, block * 8 + 8)
        real = total([near[k, rows, :cells] for k in range(8)]) * scale
        imag = total([near[k, rows, cells:] for k in range(8)]) * scale
        size = jnp.sqrt(real * real + imag * imag + 1.0)
        for span, part in ((slice(0, cells), real), (slice(cells, 2 * cells), imag)):
            part = part / size
            every[block, :, span] = part
            part = part.astype(BF16)
            for k in range(8):
                low[k, rows, span] = part
    own[...] = every[own_place()]


def mask_rows(near, scale):
    width = near.shape[-1]
    return pl.pallas_call(
        functools.partial(mask_kernel, scale),
        out_shape=(jax.ShapeDtypeStruct((8, 64, width), BF16), jax.ShapeDtypeStruct((8, width), F32)),
        in_specs=[VMEM],
        out_specs=(VMEM, VMEM),
        scratch_shapes=[pltpu.VMEM((8, 8, width), F32)],
        compiler_params=params(12),
        name="mask_rows",
    )(near)


def body(modes, back_first, back_second):
    cells = back_first.shape[1]
    scale_all = float(128) ** (-0.5)
    host_table = hermite_table(cells)
    table = jnp.asarray(host_table)
    columns = jnp.asarray(host_table.T.copy()).reshape(2, 4, 2, 64, ORDERS)
    (even_r, even_i), (odd_r, odd_i) = jax.tree.map(jnp.asarray, chirp_halves(cells))
    even = jnp.block([[even_r, -even_i], [even_i, even_r]]).reshape(2, 4, 2, 64, cells)
    odd = jnp.block([[odd_r, -odd_i], [odd_i, odd_r]]).reshape(2, 4, 2, 64, cells)
    back_first = back_first.reshape(2, 4, 2, 64, 2 * cells)
    back_second = back_second.reshape(2, 4, 2, 64, 2 * cells)
    got = swap_cores(first_product(modes, table, columns, back_first, True))
    keep = first_product(modes, table, columns, back_first, False)
    partial = halve_rows((keep.astype(F32) + got.astype(F32)).astype(BF16))
    width = 2 * cells
    near = exchange(jnp.broadcast_to(partial[None], (8, 64, width)), NARROW)
    low, mask_first = mask_rows(near, scale_all)
    mine = exchange(low, WIDE).reshape(64, 8, width)
    other = swap_cores(mine)
    own = spread_own(modes, table, columns, mine, even, odd)
    away, sums, diffs = arrive_away(modes, table, columns, other, even, odd, *own, back_second)
    got = swap_cores(away)
    keep = arrive_keep(even, odd, sums, diffs, back_second)
    partial = halve_rows((keep.astype(F32) + got.astype(F32)).astype(BF16))
    parts = exchange(partial.reshape(8, 8, width), NARROW)
    mask_second = soften(total(parts) * scale_all)
    return (mask_first, mask_second)


def solution(mesh):
    fine = Mesh(mesh.devices.reshape(2, 4, 2, 4, 2), AXES)
    placed = (P(AXES, None), P(AXES, None, None), P(AXES, None, None))
    return jax.shard_map(
        body, mesh=fine, in_specs=placed, out_specs=(P(AXES, None), P(AXES, None)), check_vma=False
    )
```

```python
import functools
import math

import jax
import jax.numpy as jnp
import numpy as np
from jax import lax
from jax.experimental import pallas as pl
from jax.experimental.pallas import tpu as pltpu
from jax.sharding import Mesh
from jax.sharding import PartitionSpec as P

ORDERS = 32
SPAN = 24.0
AXES = ("yh", "z", "core", "x", "yl")
BF16 = jnp.bfloat16
F32 = jnp.float32
ANY = pl.BlockSpec(memory_space=pl.ANY)
VMEM = pl.BlockSpec(memory_space=pltpu.VMEM)
SMEM = pl.BlockSpec(memory_space=pltpu.SMEM)
DMA = pltpu.SemaphoreType.DMA


def params(mib):
    return pltpu.CompilerParams(vmem_limit_bytes=mib << 20)


def hermite_table(cells):
    index = np.arange(cells, dtype=np.float32)
    points = ((index - np.float32(cells / 2) + np.float32(0.5)) * np.float32(SPAN / cells)).astype(np.float32)
    before = np.zeros_like(points)
    current = (np.float32(math.pi ** (-0.25)) * np.exp(np.float32(-0.5) * points * points)).astype(np.float32)
    collected = []
    for order in range(ORDERS):
        collected.append(current)
        following = (
            np.float32(math.sqrt(2.0 / (order + 1))) * points * current
            - np.float32(math.sqrt(order / (order + 1.0))) * before
        ).astype(np.float32)
        before, current = (current, following)
    return np.stack(collected, axis=0)


def chirp_halves(cells):
    half = cells // 2
    index = np.arange(half, dtype=np.int64)
    offset = index[:, None] - index[None, :]
    square = offset * offset % (2 * cells)
    phase = square.astype(np.float64) * (math.pi / cells)
    factor = cells ** (-0.5)
    real = (np.cos(phase) * factor).astype(np.float32)
    imag = (np.sin(phase) * factor).astype(np.float32)
    even = offset % 2 == 0
    out = []
    for keep in (even, ~even):
        r = np.where(keep, real, 0.0)
        i = np.where(keep, imag, 0.0)
        out.append((r.astype(jnp.bfloat16), i.astype(jnp.bfloat16)))
    return out


def soften(intersection):
    half = intersection.shape[-1] // 2
    real_part = intersection[..., :half]
    imag_part = intersection[..., half:]
    denom = jnp.sqrt(real_part * real_part + imag_part * imag_part + 1.0)
    return intersection / jnp.concatenate([denom, denom], axis=-1)


def swap_cores(block):
    return lax.ppermute(block, "core", [(0, 1), (1, 0)])


def row_of(modes, columns, core):
    picked = columns[:, :, core].reshape(512, ORDERS)
    lanes = lax.broadcasted_iota(jnp.int32, picked.shape, 1)
    return jnp.sum(jnp.where(lanes == modes[0, 0], picked, 0.0), axis=1, keepdims=True)


def bits_of(spot):
    return (spot & 1) ^ (spot >> 1), spot >> 1


def owner_codes():
    out = []
    for yh in range(2):
        for z in range(4):
            for x in range(4):
                for yl in range(2):
                    (ax, bx), (ay, by), (az, bz) = bits_of(x), bits_of(yh * 2 + yl), bits_of(z)
                    out.append((ax * 4 + ay * 2 + az, bx * 4 + by * 2 + bz))
    return out


CODES = owner_codes()


def place_of(block, core):
    a, b = CODES[block]
    return a * 8 + b + core * (7 * b - 7 * a)


def device_groups():
    def device(a, b, core):
        x, y, z = ((a >> k & 1) ^ (3 * (b >> k & 1)) for k in (2, 1, 0))
        return ((((y >> 1) * 4 + z) * 2 + core) * 4 + x) * 2 + (y & 1)

    over_a = [[[device(a, b, core) for a in range(8)] for b in range(8)] for core in range(2)]
    over_b = [[[device(a, b, core) for b in range(8)] for a in range(8)] for core in range(2)]
    return over_a[0] + over_b[1], over_b[0] + over_a[1]


WIDE, NARROW = device_groups()


def first_kernel(away, modes, table_in, columns_in, back, out, table, columns, buf, ready, loads, sems, stores):
    core = lax.axis_index("core")
    if away:
        core = 1 - core
    heads = [
        pltpu.make_async_copy(table_in, table, loads.at[0]),
        pltpu.make_async_copy(columns_in.at[:, :, core], columns.at[:, :, 0], loads.at[1]),
    ]
    copies = [
        pltpu.make_async_copy(back.at[k // 4, k % 4, core], buf.at[k], sems.at[k]) for k in range(8)
    ]
    for copy in heads + copies:
        copy.start()
    for copy in heads:
        copy.wait()
    row_func = row_of(modes, columns, 0)
    col_func = table[pl.ds(modes[0, 1], 1), :]
    cells = col_func.shape[1]
    sent = []
    for k in range(8):
        copies[k].wait()
        for j in range(8):
            block = k * 8 + j
            field = (row_func[block * 8 : block * 8 + 8] * col_func).astype(BF16).astype(F32)
            for plane in range(2):
                span = slice(plane * cells, (plane + 1) * cells)
                ready[block, :, span] = (buf[k, j * 8 : j * 8 + 8, span].astype(F32) * field).astype(BF16)
            copy = pltpu.make_async_copy(ready.at[block], out.at[place_of(block, core)], stores.at[block])
            copy.start()
            sent.append(copy)
    for copy in sent:
        copy.wait()


def first_product(modes, table, columns, back, away):
    width = back.shape[-1]
    return pl.pallas_call(
        functools.partial(first_kernel, away),
        out_shape=jax.ShapeDtypeStruct((64, 8, width), BF16),
        in_specs=[SMEM, ANY, ANY, ANY],
        out_specs=ANY,
        scratch_shapes=[
            pltpu.VMEM(table.shape, F32),
            pltpu.VMEM((2, 4, 1, 64, ORDERS), F32),
            pltpu.VMEM((8, 64, width), BF16),
            pltpu.VMEM((64, 8, width), BF16),
            DMA((2,)),
            DMA((8,)),
            DMA((64,)),
        ],
        compiler_params=params(60 if away else 14),
        cost_estimate=pl.CostEstimate(flops=2 << 20, bytes_accessed=4 << 20, transcendentals=0),
        name="first_away" if away else "first_keep",
    )(modes, table, columns, back)


def spread_half(modes, table, columns, mask, even, odd, plus, minus, sums, diffs, core, slot):
    row_func = row_of(modes, columns, core)
    col_func = table[pl.ds(modes[0, 1], 1), :]
    cells = col_func.shape[1]
    half = cells // 2
    for pair in range(32):
        kept = []
        for block in (2 * pair, 2 * pair + 1):
            place = place_of(block, core)
            field = (row_func[block * 8 : block * 8 + 8] * col_func).astype(BF16).astype(F32)
            kept.append((mask[place, :, :cells].astype(F32) * field, mask[place, :, cells:].astype(F32) * (-field)))
        rows = slice(pair * 16, pair * 16 + 16)
        real, imag = (jnp.concatenate([kept[0][k], kept[1][k]], axis=0) for k in range(2))
        for keep, sign in ((plus, 1.0), (minus, -1.0)):
            p = real[:, :half] + sign * real[:, half:]
            q = imag[:, :half] + sign * imag[:, half:]
            for k, part in enumerate((p + q, p, q)):
                keep[rows, k * half : (k + 1) * half] = part.astype(BF16)
    for n in range(2):
        span = slice(n * 256, (n + 1) * 256)
        sides = []
        for keep, chirp in ((plus, even), (minus, odd)):
            both, p, q = (
                jnp.dot(keep[:, k * half : (k + 1) * half], chirp[k, :, span], preferred_element_type=F32)
                for k in range(3)
            )
            sides.append((both + q, p - both))
        for plane in range(2):
            e, o = sides[0][plane], sides[1][plane]
            for shift, value in ((0, e + o), (half, e - o)):
                value = value.astype(BF16)
                top, bottom = value[:256], value[256:]
                where = slice(n * 256 + shift, n * 256 + shift + 256)
                sums[plane, :, slot, :, where] = (top + bottom).reshape(4, 64, 256)
                diffs[plane, :, slot, :, where] = (top - bottom).reshape(4, 64, 256)


def second_half(even, odd, sums, diffs, back, out, core):
    cells = sums.shape[-1]
    rows_even = even[:, :, core].reshape(512, cells)
    rows_odd = odd[:, :, core].reshape(512, cells)
    for n in range(4):
        span = slice(n * 256, (n + 1) * 256)
        e = jnp.dot(rows_even, sums[:, :, :, :, span].reshape(cells, 256), preferred_element_type=F32)
        o = jnp.dot(rows_odd, diffs[:, :, :, :, span].reshape(cells, 256), preferred_element_type=F32)
        other = slice(cells + n * 256, cells + (n + 1) * 256)
        for h, value in ((0, e + o), (1, e - o)):
            real, imag = value[:256], value[256:]
            back_real = back[h, :, :, span].reshape(256, 256).astype(F32)
            back_imag = back[h, :, :, other].reshape(256, 256).astype(F32)
            new_real = back_real * real + back_imag * imag
            new_imag = back_imag * real - back_real * imag
            for j in range(32):
                place = place_of(h * 32 + j, core)
                out[place, :, span] = new_real[j * 8 : j * 8 + 8].astype(BF16)
                out[place, :, other] = new_imag[j * 8 : j * 8 + 8].astype(BF16)


def spread_kernel(modes, table, columns, mask, even, odd, sums, diffs, plus, minus):
    core = lax.axis_index("core")
    spread_half(modes, table, columns, mask, even, odd, plus, minus, sums, diffs, core, 0)


def spread_own(modes, table, columns, mask, even, odd):
    cells = table.shape[-1]
    shape = jax.ShapeDtypeStruct((2, 4, 1, 64, cells), BF16)
    return pl.pallas_call(
        spread_kernel,
        out_shape=(shape, shape),
        in_specs=[SMEM] + [VMEM] * 5,
        out_specs=(VMEM, VMEM),
        scratch_shapes=[pltpu.VMEM((512, 3 * cells // 2), BF16)] * 2,
        compiler_params=params(20),
        name="spread_own",
    )(modes, table, columns, mask, even, odd)


def arrive_kernel(
    modes, table, columns, mask, even, odd, left_even, left_odd, own_sums, own_diffs, back,
    out, sums, diffs, buf, plus, minus, sem,
):
    core = lax.axis_index("core")
    other = 1 - core
    copy = pltpu.make_async_copy(back.at[:, :, other], buf, sem)
    copy.start()
    spread_half(modes, table, columns, mask, even, odd, plus, minus, sums, diffs, other, other)
    sums[:, :, core] = own_sums[:, :, 0]
    diffs[:, :, core] = own_diffs[:, :, 0]
    copy.wait()
    second_half(left_even, left_odd, sums, diffs, buf, out, other)


def arrive_away(modes, table, columns, mask, even, odd, left_even, left_odd, own_sums, own_diffs, back):
    width = back.shape[-1]
    cells = width // 2
    shape = jax.ShapeDtypeStruct((2, 4, 2, 64, cells), BF16)
    return pl.pallas_call(
        arrive_kernel,
        out_shape=(jax.ShapeDtypeStruct((64, 8, width), BF16), shape, shape),
        in_specs=[SMEM] + [VMEM] * 9 + [ANY],
        out_specs=(VMEM, VMEM, VMEM),
        scratch_shapes=[pltpu.VMEM((2, 4, 64, width), BF16)] + [pltpu.VMEM((512, 3 * cells // 2), BF16)] * 2 + [DMA],
        compiler_params=params(32),
        name="arrive_away",
    )(modes, table, columns, mask, even, odd, left_even, left_odd, own_sums, own_diffs, back)


def keep_kernel(even, odd, sums, diffs, back, out, buf, sem):
    core = lax.axis_index("core")
    copy = pltpu.make_async_copy(back.at[:, :, core], buf, sem)
    copy.start()
    copy.wait()
    second_half(even, odd, sums, diffs, buf, out, core)


def arrive_keep(even, odd, sums, diffs, back):
    width = back.shape[-1]
    return pl.pallas_call(
        keep_kernel,
        out_shape=jax.ShapeDtypeStruct((64, 8, width), BF16),
        in_specs=[VMEM] * 4 + [ANY],
        out_specs=VMEM,
        scratch_shapes=[pltpu.VMEM((2, 4, 64, width), BF16), DMA],
        compiler_params=params(20),
        name="arrive_keep",
    )(even, odd, sums, diffs, back)


def exchange(blocks, groups):
    return lax.all_to_all(blocks, AXES, 0, 0, tiled=True, axis_index_groups=groups)


def total(parts):
    kept = [parts[k].astype(F32) for k in range(len(parts))]
    while len(kept) > 1:
        kept = [kept[k] + kept[k + 1] for k in range(0, len(kept), 2)]
    return kept[0]


def halve_rows(both):
    width = both.shape[-1]
    return total(exchange(both.reshape(8, 64, width), WIDE)).astype(BF16)


def own_place():
    pairs = [bits_of(lax.axis_index("x")), bits_of(lax.axis_index("yh") * 2 + lax.axis_index("yl"))]
    pairs.append(bits_of(lax.axis_index("z")))
    a, b = (pairs[0][k] * 4 + pairs[1][k] * 2 + pairs[2][k] for k in range(2))
    return b + lax.axis_index("core") * (a - b)


def mask_kernel(scale, near, low, own, every):
    cells = near.shape[-1] // 2
    for block in range(8):
        rows = slice(block * 8, block * 8 + 8)
        real = total([near[k, rows, :cells] for k in range(8)]) * scale
        imag = total([near[k, rows, cells:] for k in range(8)]) * scale
        size = jnp.sqrt(real * real + imag * imag + 1.0)
        for span, part in ((slice(0, cells), real), (slice(cells, 2 * cells), imag)):
            part = part / size
            every[block, :, span] = part
            part = part.astype(BF16)
            for k in range(8):
                low[k, rows, span] = part
    own[...] = every[own_place()]


def mask_rows(near, scale):
    width = near.shape[-1]
    return pl.pallas_call(
        functools.partial(mask_kernel, scale),
        out_shape=(jax.ShapeDtypeStruct((8, 64, width), BF16), jax.ShapeDtypeStruct((8, width), F32)),
        in_specs=[VMEM],
        out_specs=(VMEM, VMEM),
        scratch_shapes=[pltpu.VMEM((8, 8, width), F32)],
        compiler_params=params(12),
        name="mask_rows",
    )(near)


def body(modes, back_first, back_second):
    cells = back_first.shape[1]
    scale_all = float(128) ** (-0.5)
    host_table = hermite_table(cells)
    table = jnp.asarray(host_table)
    columns = jnp.asarray(host_table.T.copy()).reshape(2, 4, 2, 64, ORDERS)
    left, right = [], []
    for r, i in chirp_halves(cells):
        left.append(jnp.asarray(np.block([[r, -i], [i, r]])).reshape(2, 4, 2, 64, cells))
        wide_r, wide_i = r.astype(np.float32), i.astype(np.float32)
        right.append(jnp.asarray(np.stack([r, (wide_r + wide_i).astype(r.dtype), (wide_i - wide_r).astype(r.dtype)])))
    back_first = back_first.reshape(2, 4, 2, 64, 2 * cells)
    back_second = back_second.reshape(2, 4, 2, 64, 2 * cells)
    got = swap_cores(first_product(modes, table, columns, back_first, True))
    keep = first_product(modes, table, columns, back_first, False)
    partial = halve_rows((keep.astype(F32) + got.astype(F32)).astype(BF16))
    width = 2 * cells
    near = exchange(jnp.broadcast_to(partial[None], (8, 64, width)), NARROW)
    low, mask_first = mask_rows(near, scale_all)
    mine = exchange(low, WIDE).reshape(64, 8, width)
    other = swap_cores(mine)
    own = spread_own(modes, table, columns, mine, *right)
    away, sums, diffs = arrive_away(modes, table, columns, other, *right, *left, *own, back_second)
    got = swap_cores(away)
    keep = arrive_keep(*left, sums, diffs, back_second)
    partial = halve_rows((keep.astype(F32) + got.astype(F32)).astype(BF16))
    parts = exchange(partial.reshape(8, 8, width), NARROW)
    mask_second = soften(total(parts) * scale_all)
    return (mask_first, mask_second)


def solution(mesh):
    fine = Mesh(mesh.devices.reshape(2, 4, 2, 4, 2), AXES)
    placed = (P(AXES, None), P(AXES, None, None), P(AXES, None, None))
    return jax.shard_map(
        body, mesh=fine, in_specs=placed, out_specs=(P(AXES, None), P(AXES, None)), check_vma=False
    )
```

```python
import functools
import math

import jax
import jax.numpy as jnp
import numpy as np
from jax import lax
from jax.experimental import pallas as pl
from jax.experimental.pallas import tpu as pltpu
from jax.sharding import Mesh
from jax.sharding import PartitionSpec as P

ORDERS = 32
SPAN = 24.0
AXES = ("yh", "z", "core", "x", "yl")
BF16 = jnp.bfloat16
F32 = jnp.float32
ANY = pl.BlockSpec(memory_space=pl.ANY)
VMEM = pl.BlockSpec(memory_space=pltpu.VMEM)
SMEM = pl.BlockSpec(memory_space=pltpu.SMEM)
DMA = pltpu.SemaphoreType.DMA


def params(mib):
    return pltpu.CompilerParams(vmem_limit_bytes=mib << 20)


def hermite_table(cells):
    index = np.arange(cells, dtype=np.float32)
    points = ((index - np.float32(cells / 2) + np.float32(0.5)) * np.float32(SPAN / cells)).astype(np.float32)
    before = np.zeros_like(points)
    current = (np.float32(math.pi ** (-0.25)) * np.exp(np.float32(-0.5) * points * points)).astype(np.float32)
    collected = []
    for order in range(ORDERS):
        collected.append(current)
        following = (
            np.float32(math.sqrt(2.0 / (order + 1))) * points * current
            - np.float32(math.sqrt(order / (order + 1.0))) * before
        ).astype(np.float32)
        before, current = (current, following)
    return np.stack(collected, axis=0)


def chirp_halves(cells):
    half = cells // 2
    index = np.arange(half, dtype=np.int64)
    offset = index[:, None] - index[None, :]
    square = offset * offset % (2 * cells)
    phase = square.astype(np.float64) * (math.pi / cells)
    factor = cells ** (-0.5)
    real = (np.cos(phase) * factor).astype(np.float32)
    imag = (np.sin(phase) * factor).astype(np.float32)
    even = offset % 2 == 0
    out = []
    for keep in (even, ~even):
        r = np.where(keep, real, 0.0)
        i = np.where(keep, imag, 0.0)
        out.append((r.astype(jnp.bfloat16), i.astype(jnp.bfloat16)))
    return out


def soften(intersection):
    half = intersection.shape[-1] // 2
    real_part = intersection[..., :half]
    imag_part = intersection[..., half:]
    denom = jnp.sqrt(real_part * real_part + imag_part * imag_part + 1.0)
    return intersection / jnp.concatenate([denom, denom], axis=-1)


def swap_cores(block):
    return lax.ppermute(block, "core", [(0, 1), (1, 0)])


def row_of(modes, columns, core):
    picked = columns[:, :, core].reshape(512, ORDERS)
    lanes = lax.broadcasted_iota(jnp.int32, picked.shape, 1)
    return jnp.sum(jnp.where(lanes == modes[0, 0], picked, 0.0), axis=1, keepdims=True)


def bits_of(spot):
    return (spot & 1) ^ (spot >> 1), spot >> 1


def owner_codes():
    out = []
    for yh in range(2):
        for z in range(4):
            for x in range(4):
                for yl in range(2):
                    (ax, bx), (ay, by), (az, bz) = bits_of(x), bits_of(yh * 2 + yl), bits_of(z)
                    out.append((ax * 4 + ay * 2 + az, bx * 4 + by * 2 + bz))
    return out


CODES = owner_codes()


def place_of(block, core):
    a, b = CODES[block]
    return a * 8 + b + core * (7 * b - 7 * a)


def device_groups():
    def device(a, b, core):
        x, y, z = ((a >> k & 1) ^ (3 * (b >> k & 1)) for k in (2, 1, 0))
        return ((((y >> 1) * 4 + z) * 2 + core) * 4 + x) * 2 + (y & 1)

    over_a = [[[device(a, b, core) for a in range(8)] for b in range(8)] for core in range(2)]
    over_b = [[[device(a, b, core) for b in range(8)] for a in range(8)] for core in range(2)]
    return over_a[0] + over_b[1], over_b[0] + over_a[1]


WIDE, NARROW = device_groups()


def first_kernel(away, modes, table_in, columns_in, back, out, table, columns, buf, loads, sems):
    core = lax.axis_index("core")
    if away:
        core = 1 - core
    heads = [
        pltpu.make_async_copy(table_in, table, loads.at[0]),
        pltpu.make_async_copy(columns_in.at[:, :, core], columns.at[:, :, 0], loads.at[1]),
    ]
    copies = [
        pltpu.make_async_copy(back.at[k // 4, k % 4, core], buf.at[k], sems.at[k]) for k in range(8)
    ]
    for copy in heads + copies:
        copy.start()
    for copy in heads:
        copy.wait()
    row_func = row_of(modes, columns, 0)
    col_func = table[pl.ds(modes[0, 1], 1), :]
    cells = col_func.shape[1]
    for k in range(8):
        copies[k].wait()
        for j in range(8):
            block = k * 8 + j
            place = place_of(block, core)
            field = (row_func[block * 8 : block * 8 + 8] * col_func).astype(BF16)
            for plane in range(2):
                span = slice(plane * cells, (plane + 1) * cells)
                out[place, :, span] = buf[k, j * 8 : j * 8 + 8, span] * field


def first_product(modes, table, columns, back, away):
    width = back.shape[-1]
    return pl.pallas_call(
        functools.partial(first_kernel, away),
        out_shape=jax.ShapeDtypeStruct((64, 8, width), BF16),
        in_specs=[SMEM, ANY, ANY, ANY],
        out_specs=VMEM,
        scratch_shapes=[
            pltpu.VMEM(table.shape, F32),
            pltpu.VMEM((2, 4, 1, 64, ORDERS), F32),
            pltpu.VMEM((8, 64, width), BF16),
            DMA((2,)),
            DMA((8,)),
        ],
        compiler_params=params(60 if away else 14),
        cost_estimate=pl.CostEstimate(flops=2 << 20, bytes_accessed=4 << 20, transcendentals=0),
        name="first_away" if away else "first_keep",
    )(modes, table, columns, back)


def spread_half(modes, table, columns, mask, even, odd, plus, minus, sums, diffs, core, slot):
    row_func = row_of(modes, columns, core)
    col_func = table[pl.ds(modes[0, 1], 1), :]
    cells = col_func.shape[1]
    half = cells // 2
    for pair in range(32):
        first, second = (mask[place_of(2 * pair + k, core)] for k in range(2))
        both = jnp.concatenate([first, second], axis=0)
        rows = slice(pair * 16, pair * 16 + 16)
        field = (row_func[rows] * col_func).astype(BF16)
        for plane, value in ((0, both[:, :cells] * field), (1, both[:, cells:] * (-field))):
            span = slice(plane * half, (plane + 1) * half)
            plus[rows, span] = value[:, :half] + value[:, half:]
            minus[rows, span] = value[:, :half] - value[:, half:]
    for n in range(4):
        span = slice(n * 256, (n + 1) * 256)
        e = jnp.dot(plus[...], even[:, :, :, :, span].reshape(cells, 256), preferred_element_type=F32)
        o = jnp.dot(minus[...], odd[:, :, :, :, span].reshape(cells, 256), preferred_element_type=F32)
        plane, at = n // 2, (n % 2) * 256
        for shift, value in ((0, e + o), (half, e - o)):
            value = (-value if plane else value).astype(BF16)
            top, bottom = value[:256], value[256:]
            where = slice(at + shift, at + shift + 256)
            sums[plane, :, slot, :, where] = (top + bottom).reshape(4, 64, 256)
            diffs[plane, :, slot, :, where] = (top - bottom).reshape(4, 64, 256)


def second_half(even, odd, sums, diffs, back, out, core):
    cells = sums.shape[-1]
    rows_even = even[:, :, core].reshape(512, cells)
    rows_odd = odd[:, :, core].reshape(512, cells)
    for n in range(4):
        span = slice(n * 256, (n + 1) * 256)
        other = slice(cells + n * 256, cells + (n + 1) * 256)
        right_even = sums[:, :, :, :, span].reshape(cells, 256)
        right_odd = diffs[:, :, :, :, span].reshape(cells, 256)
        e, o = (
            [jnp.dot(rows[k * 256 : k * 256 + 256], right, preferred_element_type=F32) for k in range(2)]
            for rows, right in ((rows_even, right_even), (rows_odd, right_odd))
        )
        for j in range(32):
            for h in range(2):
                at = slice(j * 8, j * 8 + 8)
                real = e[0][at] - o[0][at] if h else e[0][at] + o[0][at]
                imag = e[1][at] - o[1][at] if h else e[1][at] + o[1][at]
                back_real = back[h, j // 8, j % 8 * 8 : j % 8 * 8 + 8, span].astype(F32)
                back_imag = back[h, j // 8, j % 8 * 8 : j % 8 * 8 + 8, other].astype(F32)
                place = place_of(h * 32 + j, core)
                out[place, :, span] = (back_real * real + back_imag * imag).astype(BF16)
                out[place, :, other] = (back_imag * real - back_real * imag).astype(BF16)


def spread_kernel(modes, table, columns, mask, even, odd, sums, diffs, plus, minus):
    core = lax.axis_index("core")
    spread_half(modes, table, columns, mask, even, odd, plus, minus, sums, diffs, core, 0)


def spread_own(modes, table, columns, mask, even, odd):
    cells = even.shape[-1]
    shape = jax.ShapeDtypeStruct((2, 4, 1, 64, cells), BF16)
    return pl.pallas_call(
        spread_kernel,
        out_shape=(shape, shape),
        in_specs=[SMEM] + [VMEM] * 5,
        out_specs=(VMEM, VMEM),
        scratch_shapes=[pltpu.VMEM((512, cells), BF16)] * 2,
        compiler_params=params(20),
        name="spread_own",
    )(modes, table, columns, mask, even, odd)


def arrive_kernel(
    modes, table, columns, mask, even, odd, own_sums, own_diffs, back, out, sums, diffs, buf, plus, minus, sem
):
    core = lax.axis_index("core")
    other = 1 - core
    copy = pltpu.make_async_copy(back.at[:, :, other], buf, sem)
    copy.start()
    spread_half(modes, table, columns, mask, even, odd, plus, minus, sums, diffs, other, other)
    sums[:, :, core] = own_sums[:, :, 0]
    diffs[:, :, core] = own_diffs[:, :, 0]
    copy.wait()
    second_half(even, odd, sums, diffs, buf, out, other)


def arrive_away(modes, table, columns, mask, even, odd, own_sums, own_diffs, back):
    width = back.shape[-1]
    cells = width // 2
    shape = jax.ShapeDtypeStruct((2, 4, 2, 64, cells), BF16)
    return pl.pallas_call(
        arrive_kernel,
        out_shape=(jax.ShapeDtypeStruct((64, 8, width), BF16), shape, shape),
        in_specs=[SMEM] + [VMEM] * 7 + [ANY],
        out_specs=(VMEM, VMEM, VMEM),
        scratch_shapes=[pltpu.VMEM((2, 4, 64, width), BF16)] + [pltpu.VMEM((512, cells), BF16)] * 2 + [DMA],
        compiler_params=params(28),
        name="arrive_away",
    )(modes, table, columns, mask, even, odd, own_sums, own_diffs, back)


def keep_kernel(even, odd, sums, diffs, back, out, buf, sem):
    core = lax.axis_index("core")
    copy = pltpu.make_async_copy(back.at[:, :, core], buf, sem)
    copy.start()
    copy.wait()
    second_half(even, odd, sums, diffs, buf, out, core)


def arrive_keep(even, odd, sums, diffs, back):
    width = back.shape[-1]
    return pl.pallas_call(
        keep_kernel,
        out_shape=jax.ShapeDtypeStruct((64, 8, width), BF16),
        in_specs=[VMEM] * 4 + [ANY],
        out_specs=VMEM,
        scratch_shapes=[pltpu.VMEM((2, 4, 64, width), BF16), DMA],
        compiler_params=params(20),
        name="arrive_keep",
    )(even, odd, sums, diffs, back)


def exchange(blocks, groups):
    return lax.all_to_all(blocks, AXES, 0, 0, tiled=True, axis_index_groups=groups)


def total(parts):
    kept = [parts[k].astype(F32) for k in range(len(parts))]
    while len(kept) > 1:
        kept = [kept[k] + kept[k + 1] for k in range(0, len(kept), 2)]
    return kept[0]


def halve_rows(both):
    width = both.shape[-1]
    return total(exchange(both.reshape(8, 64, width), WIDE)).astype(BF16)


def own_place():
    pairs = [bits_of(lax.axis_index("x")), bits_of(lax.axis_index("yh") * 2 + lax.axis_index("yl"))]
    pairs.append(bits_of(lax.axis_index("z")))
    a, b = (pairs[0][k] * 4 + pairs[1][k] * 2 + pairs[2][k] for k in range(2))
    return b + lax.axis_index("core") * (a - b)


def mask_kernel(scale, near, low, own, every):
    cells = near.shape[-1] // 2
    for block in range(8):
        rows = slice(block * 8, block * 8 + 8)
        real = total([near[k, rows, :cells] for k in range(8)]) * scale
        imag = total([near[k, rows, cells:] for k in range(8)]) * scale
        size = jnp.sqrt(real * real + imag * imag + 1.0)
        for span, part in ((slice(0, cells), real), (slice(cells, 2 * cells), imag)):
            part = part / size
            every[block, :, span] = part
            part = part.astype(BF16)
            for k in range(8):
                low[k, rows, span] = part
    own[...] = every[own_place()]


def mask_rows(near, scale):
    width = near.shape[-1]
    return pl.pallas_call(
        functools.partial(mask_kernel, scale),
        out_shape=(jax.ShapeDtypeStruct((8, 64, width), BF16), jax.ShapeDtypeStruct((8, width), F32)),
        in_specs=[VMEM],
        out_specs=(VMEM, VMEM),
        scratch_shapes=[pltpu.VMEM((8, 8, width), F32)],
        compiler_params=params(12),
        name="mask_rows",
    )(near)


def body(modes, back_first, back_second):
    cells = back_first.shape[1]
    scale_all = float(128) ** (-0.5)
    host_table = hermite_table(cells)
    table = jnp.asarray(host_table)
    columns = jnp.asarray(host_table.T.copy()).reshape(2, 4, 2, 64, ORDERS)
    (even_r, even_i), (odd_r, odd_i) = jax.tree.map(jnp.asarray, chirp_halves(cells))
    even = jnp.block([[even_r, -even_i], [even_i, even_r]]).reshape(2, 4, 2, 64, cells)
    odd = jnp.block([[odd_r, -odd_i], [odd_i, odd_r]]).reshape(2, 4, 2, 64, cells)
    back_first = back_first.reshape(2, 4, 2, 64, 2 * cells)
    back_second = back_second.reshape(2, 4, 2, 64, 2 * cells)
    got = swap_cores(first_product(modes, table, columns, back_first, True))
    keep = first_product(modes, table, columns, back_first, False)
    partial = halve_rows((keep.astype(F32) + got.astype(F32)).astype(BF16))
    width = 2 * cells
    near = exchange(jnp.broadcast_to(partial[None], (8, 64, width)), NARROW)
    low, mask_first = mask_rows(near, scale_all)
    mine = exchange(low, WIDE).reshape(64, 8, width)
    other = swap_cores(mine)
    own = spread_own(modes, table, columns, mine, even, odd)
    away, sums, diffs = arrive_away(modes, table, columns, other, even, odd, *own, back_second)
    got = swap_cores(away)
    keep = arrive_keep(even, odd, sums, diffs, back_second)
    partial = halve_rows((keep.astype(F32) + got.astype(F32)).astype(BF16))
    parts = exchange(partial.reshape(8, 8, width), NARROW)
    mask_second = soften(total(parts) * scale_all)
    return (mask_first, mask_second)


def solution(mesh):
    fine = Mesh(mesh.devices.reshape(2, 4, 2, 4, 2), AXES)
    placed = (P(AXES, None), P(AXES, None, None), P(AXES, None, None))
    return jax.shard_map(
        body, mesh=fine, in_specs=placed, out_specs=(P(AXES, None), P(AXES, None)), check_vma=False
    )
```

```python
import functools
import math

import jax
import jax.numpy as jnp
import numpy as np
from jax import lax
from jax.experimental import pallas as pl
from jax.experimental.pallas import tpu as pltpu
from jax.sharding import Mesh
from jax.sharding import PartitionSpec as P

ORDERS = 32
SPAN = 24.0
AXES = ("yh", "z", "core", "x", "yl")
BF16 = jnp.bfloat16
F32 = jnp.float32
ANY = pl.BlockSpec(memory_space=pl.ANY)
VMEM = pl.BlockSpec(memory_space=pltpu.VMEM)
SMEM = pl.BlockSpec(memory_space=pltpu.SMEM)
DMA = pltpu.SemaphoreType.DMA


def params(mib):
    return pltpu.CompilerParams(vmem_limit_bytes=mib << 20)


def hermite_table(cells):
    index = np.arange(cells, dtype=np.float32)
    points = ((index - np.float32(cells / 2) + np.float32(0.5)) * np.float32(SPAN / cells)).astype(np.float32)
    before = np.zeros_like(points)
    current = (np.float32(math.pi ** (-0.25)) * np.exp(np.float32(-0.5) * points * points)).astype(np.float32)
    collected = []
    for order in range(ORDERS):
        collected.append(current)
        following = (
            np.float32(math.sqrt(2.0 / (order + 1))) * points * current
            - np.float32(math.sqrt(order / (order + 1.0))) * before
        ).astype(np.float32)
        before, current = (current, following)
    return np.stack(collected, axis=0)


def chirp_halves(cells):
    half = cells // 2
    index = np.arange(half, dtype=np.int64)
    offset = index[:, None] - index[None, :]
    square = offset * offset % (2 * cells)
    phase = square.astype(np.float64) * (math.pi / cells)
    factor = cells ** (-0.5)
    real = (np.cos(phase) * factor).astype(np.float32)
    imag = (np.sin(phase) * factor).astype(np.float32)
    even = offset % 2 == 0
    out = []
    for keep in (even, ~even):
        r = np.where(keep, real, 0.0)
        i = np.where(keep, imag, 0.0)
        out.append((r.astype(jnp.bfloat16), i.astype(jnp.bfloat16)))
    return out


def soften(intersection):
    half = intersection.shape[-1] // 2
    real_part = intersection[..., :half]
    imag_part = intersection[..., half:]
    denom = jnp.sqrt(real_part * real_part + imag_part * imag_part + 1.0)
    return intersection / jnp.concatenate([denom, denom], axis=-1)


def swap_cores(block):
    return lax.ppermute(block, "core", [(0, 1), (1, 0)])


def row_of(modes, columns, core):
    picked = columns[:, :, core].reshape(512, ORDERS)
    lanes = lax.broadcasted_iota(jnp.int32, picked.shape, 1)
    return jnp.sum(jnp.where(lanes == modes[0, 0], picked, 0.0), axis=1, keepdims=True)


def bits_of(spot):
    return (spot & 1) ^ (spot >> 1), spot >> 1


def owner_codes():
    out = []
    for yh in range(2):
        for z in range(4):
            for x in range(4):
                for yl in range(2):
                    (ax, bx), (ay, by), (az, bz) = bits_of(x), bits_of(yh * 2 + yl), bits_of(z)
                    out.append((ax * 4 + ay * 2 + az, bx * 4 + by * 2 + bz))
    return out


CODES = owner_codes()


def place_of(block, core):
    a, b = CODES[block]
    return a * 8 + b + core * (7 * b - 7 * a)


def device_groups():
    def device(a, b, core):
        x, y, z = ((a >> k & 1) ^ (3 * (b >> k & 1)) for k in (2, 1, 0))
        return ((((y >> 1) * 4 + z) * 2 + core) * 4 + x) * 2 + (y & 1)

    over_a = [[[device(a, b, core) for a in range(8)] for b in range(8)] for core in range(2)]
    over_b = [[[device(a, b, core) for b in range(8)] for a in range(8)] for core in range(2)]
    return over_a[0] + over_b[1], over_b[0] + over_a[1]


WIDE, NARROW = device_groups()


def own_kernel(modes, table, columns, back, out, buf, sems):
    core = lax.axis_index("core")
    copies = [
        pltpu.make_async_copy(back.at[k // 4, k % 4, core], buf.at[k], sems.at[k]) for k in range(8)
    ]
    for copy in copies:
        copy.start()
    row_func = row_of(modes, columns, core)
    col_func = table[pl.ds(modes[0, 1], 1), :]
    cells = table.shape[1]
    for k in range(8):
        copies[k].wait()
        for j in range(8):
            block = k * 8 + j
            field = (row_func[block * 8 : block * 8 + 8] * col_func).astype(BF16)
            for plane in range(2):
                span = slice(plane * cells, (plane + 1) * cells)
                out[place_of(block, core), :, span] = buf[k, j * 8 : j * 8 + 8, span] * field


def own_product(modes, table, columns, back):
    width = back.shape[-1]
    return pl.pallas_call(
        own_kernel,
        out_shape=jax.ShapeDtypeStruct((64, 8, width), BF16),
        in_specs=[SMEM, VMEM, VMEM, ANY],
        out_specs=VMEM,
        scratch_shapes=[pltpu.VMEM((8, 64, width), BF16), DMA((8,))],
        compiler_params=params(14),
        cost_estimate=pl.CostEstimate(flops=2 << 20, bytes_accessed=4 << 20, transcendentals=0),
        name="own_product",
    )(modes, table, columns, back)


def both_kernel(peer, table, columns, got, keep, out):
    core = lax.axis_index("core")
    row_func = row_of(peer, columns, core)
    col_func = table[pl.ds(peer[0, 1], 1), :]
    cells = table.shape[1]
    for block in range(64):
        place = place_of(block, core)
        k, j = block // 8, block % 8
        field = (row_func[block * 8 : block * 8 + 8] * col_func).astype(BF16).astype(F32)
        for plane in range(2):
            span = slice(plane * cells, (plane + 1) * cells)
            value = got[k // 4, k % 4, j * 8 : j * 8 + 8, span].astype(F32) * field
            out[place, :, span] = (value + keep[place, :, span].astype(F32)).astype(BF16)


def both_products(peer, table, columns, got, keep):
    return pl.pallas_call(
        both_kernel,
        out_shape=jax.ShapeDtypeStruct(keep.shape, BF16),
        in_specs=[SMEM] + [VMEM] * 4,
        out_specs=VMEM,
        compiler_params=params(14),
        name="both_products",
    )(peer, table, columns, got, keep)


def spread_half(modes, table, columns, mask, even, odd, plus, minus, sums, diffs, core, slot):
    row_func = row_of(modes, columns, core)
    col_func = table[pl.ds(modes[0, 1], 1), :]
    cells = col_func.shape[1]
    half = cells // 2
    for pair in range(32):
        first, second = (mask[place_of(2 * pair + k, core)] for k in range(2))
        both = jnp.concatenate([first, second], axis=0)
        rows = slice(pair * 16, pair * 16 + 16)
        field = (row_func[rows] * col_func).astype(BF16)
        for plane, value in ((0, both[:, :cells] * field), (1, both[:, cells:] * (-field))):
            span = slice(plane * half, (plane + 1) * half)
            plus[rows, span] = value[:, :half] + value[:, half:]
            minus[rows, span] = value[:, :half] - value[:, half:]
    for n in range(4):
        span = slice(n * 256, (n + 1) * 256)
        e = jnp.dot(plus[...], even[:, :, :, :, span].reshape(cells, 256), preferred_element_type=F32)
        o = jnp.dot(minus[...], odd[:, :, :, :, span].reshape(cells, 256), preferred_element_type=F32)
        plane, at = n // 2, (n % 2) * 256
        for shift, value in ((0, e + o), (half, e - o)):
            value = (-value if plane else value).astype(BF16)
            top, bottom = value[:256], value[256:]
            where = slice(at + shift, at + shift + 256)
            sums[plane, :, slot, :, where] = (top + bottom).reshape(4, 64, 256)
            diffs[plane, :, slot, :, where] = (top - bottom).reshape(4, 64, 256)


def second_half(even, odd, sums, diffs, back, out, core):
    cells = sums.shape[-1]
    rows_even = even[:, :, core].reshape(512, cells)
    rows_odd = odd[:, :, core].reshape(512, cells)
    for n in range(4):
        span = slice(n * 256, (n + 1) * 256)
        other = slice(cells + n * 256, cells + (n + 1) * 256)
        right_even = sums[:, :, :, :, span].reshape(cells, 256)
        right_odd = diffs[:, :, :, :, span].reshape(cells, 256)
        e, o = (
            [jnp.dot(rows[k * 256 : k * 256 + 256], right, preferred_element_type=F32) for k in range(2)]
            for rows, right in ((rows_even, right_even), (rows_odd, right_odd))
        )
        for j in range(32):
            for h in range(2):
                at = slice(j * 8, j * 8 + 8)
                real = e[0][at] - o[0][at] if h else e[0][at] + o[0][at]
                imag = e[1][at] - o[1][at] if h else e[1][at] + o[1][at]
                back_real = back[h, j // 8, j % 8 * 8 : j % 8 * 8 + 8, span].astype(F32)
                back_imag = back[h, j // 8, j % 8 * 8 : j % 8 * 8 + 8, other].astype(F32)
                place = place_of(h * 32 + j, core)
                out[place, :, span] = (back_real * real + back_imag * imag).astype(BF16)
                out[place, :, other] = (back_imag * real - back_real * imag).astype(BF16)


def spread_kernel(modes, table, columns, mask, even, odd, sums, diffs, plus, minus):
    core = lax.axis_index("core")
    spread_half(modes, table, columns, mask, even, odd, plus, minus, sums, diffs, core, 0)


def spread_own(modes, table, columns, mask, even, odd):
    cells = even.shape[-1]
    shape = jax.ShapeDtypeStruct((2, 4, 1, 64, cells), BF16)
    return pl.pallas_call(
        spread_kernel,
        out_shape=(shape, shape),
        in_specs=[SMEM] + [VMEM] * 5,
        out_specs=(VMEM, VMEM),
        scratch_shapes=[pltpu.VMEM((512, cells), BF16)] * 2,
        compiler_params=params(20),
        name="spread_own",
    )(modes, table, columns, mask, even, odd)


def arrive_kernel(
    modes, table, columns, mask, even, odd, own_sums, own_diffs, back, out, sums, diffs, buf, plus, minus, sem
):
    core = lax.axis_index("core")
    other = 1 - core
    copy = pltpu.make_async_copy(back.at[:, :, other], buf, sem)
    copy.start()
    spread_half(modes, table, columns, mask, even, odd, plus, minus, sums, diffs, other, other)
    sums[:, :, core] = own_sums[:, :, 0]
    diffs[:, :, core] = own_diffs[:, :, 0]
    copy.wait()
    second_half(even, odd, sums, diffs, buf, out, other)


def arrive_away(modes, table, columns, mask, even, odd, own_sums, own_diffs, back):
    width = back.shape[-1]
    cells = width // 2
    shape = jax.ShapeDtypeStruct((2, 4, 2, 64, cells), BF16)
    return pl.pallas_call(
        arrive_kernel,
        out_shape=(jax.ShapeDtypeStruct((64, 8, width), BF16), shape, shape),
        in_specs=[SMEM] + [VMEM] * 7 + [ANY],
        out_specs=(VMEM, VMEM, VMEM),
        scratch_shapes=[pltpu.VMEM((2, 4, 64, width), BF16)] + [pltpu.VMEM((512, cells), BF16)] * 2 + [DMA],
        compiler_params=params(28),
        name="arrive_away",
    )(modes, table, columns, mask, even, odd, own_sums, own_diffs, back)


def keep_kernel(even, odd, sums, diffs, back, out, buf, sem):
    core = lax.axis_index("core")
    copy = pltpu.make_async_copy(back.at[:, :, core], buf, sem)
    copy.start()
    copy.wait()
    second_half(even, odd, sums, diffs, buf, out, core)


def arrive_keep(even, odd, sums, diffs, back):
    width = back.shape[-1]
    return pl.pallas_call(
        keep_kernel,
        out_shape=jax.ShapeDtypeStruct((64, 8, width), BF16),
        in_specs=[VMEM] * 4 + [ANY],
        out_specs=VMEM,
        scratch_shapes=[pltpu.VMEM((2, 4, 64, width), BF16), DMA],
        compiler_params=params(20),
        name="arrive_keep",
    )(even, odd, sums, diffs, back)


def exchange(blocks, groups):
    return lax.all_to_all(blocks, AXES, 0, 0, tiled=True, axis_index_groups=groups)


def total(parts):
    kept = [parts[k].astype(F32) for k in range(len(parts))]
    while len(kept) > 1:
        kept = [kept[k] + kept[k + 1] for k in range(0, len(kept), 2)]
    return kept[0]


def halve_rows(both):
    width = both.shape[-1]
    return total(exchange(both.reshape(8, 64, width), WIDE)).astype(BF16)


def own_place():
    pairs = [bits_of(lax.axis_index("x")), bits_of(lax.axis_index("yh") * 2 + lax.axis_index("yl"))]
    pairs.append(bits_of(lax.axis_index("z")))
    a, b = (pairs[0][k] * 4 + pairs[1][k] * 2 + pairs[2][k] for k in range(2))
    return b + lax.axis_index("core") * (a - b)


def mask_kernel(scale, near, low, own, every):
    cells = near.shape[-1] // 2
    for block in range(8):
        rows = slice(block * 8, block * 8 + 8)
        real = total([near[k, rows, :cells] for k in range(8)]) * scale
        imag = total([near[k, rows, cells:] for k in range(8)]) * scale
        inverse = 1.0 / jnp.sqrt(real * real + imag * imag + 1.0)
        for span, part in ((slice(0, cells), real), (slice(cells, 2 * cells), imag)):
            part = part * inverse
            every[block, :, span] = part
            part = part.astype(BF16)
            for k in range(8):
                low[k, rows, span] = part
    own[...] = every[own_place()]


def mask_rows(near, scale):
    width = near.shape[-1]
    return pl.pallas_call(
        functools.partial(mask_kernel, scale),
        out_shape=(jax.ShapeDtypeStruct((8, 64, width), BF16), jax.ShapeDtypeStruct((8, width), F32)),
        in_specs=[VMEM],
        out_specs=(VMEM, VMEM),
        scratch_shapes=[pltpu.VMEM((8, 8, width), F32)],
        compiler_params=params(12),
        name="mask_rows",
    )(near)


def body(modes, back_first, back_second):
    cells = back_first.shape[1]
    scale_all = float(128) ** (-0.5)
    host_table = hermite_table(cells)
    table = jnp.asarray(host_table)
    columns = jnp.asarray(host_table.T.copy()).reshape(2, 4, 2, 64, ORDERS)
    (even_r, even_i), (odd_r, odd_i) = jax.tree.map(jnp.asarray, chirp_halves(cells))
    even = jnp.block([[even_r, -even_i], [even_i, even_r]]).reshape(2, 4, 2, 64, cells)
    odd = jnp.block([[odd_r, -odd_i], [odd_i, odd_r]]).reshape(2, 4, 2, 64, cells)
    back_first = back_first.reshape(2, 4, 2, 64, 2 * cells)
    back_second = back_second.reshape(2, 4, 2, 64, 2 * cells)
    peer = swap_cores(modes)
    away = lax.dynamic_index_in_dim(back_first, 1 - lax.axis_index("core"), 2, keepdims=False)
    got = swap_cores(away)
    keep = own_product(modes, table, columns, back_first)
    partial = halve_rows(both_products(peer, table, columns, got, keep))
    width = 2 * cells
    near = exchange(jnp.broadcast_to(partial[None], (8, 64, width)), NARROW)
    low, mask_first = mask_rows(near, scale_all)
    mine = exchange(low, WIDE).reshape(64, 8, width)
    other = swap_cores(mine)
    own = spread_own(modes, table, columns, mine, even, odd)
    away, sums, diffs = arrive_away(modes, table, columns, other, even, odd, *own, back_second)
    got = swap_cores(away)
    keep = arrive_keep(even, odd, sums, diffs, back_second)
    partial = halve_rows((keep.astype(F32) + got.astype(F32)).astype(BF16))
    parts = exchange(partial.reshape(8, 8, width), NARROW)
    mask_second = soften(total(parts) * scale_all)
    return (mask_first, mask_second)


def solution(mesh):
    fine = Mesh(mesh.devices.reshape(2, 4, 2, 4, 2), AXES)
    placed = (P(AXES, None), P(AXES, None, None), P(AXES, None, None))
    return jax.shard_map(
        body, mesh=fine, in_specs=placed, out_specs=(P(AXES, None), P(AXES, None)), check_vma=False
    )
```

```python
import functools
import math

import jax
import jax.numpy as jnp
import numpy as np
from jax import lax
from jax.experimental import pallas as pl
from jax.experimental.pallas import tpu as pltpu
from jax.sharding import Mesh
from jax.sharding import PartitionSpec as P

ORDERS = 32
SPAN = 24.0
AXES = ("yh", "z", "core", "x", "yl")
BF16 = jnp.bfloat16
F32 = jnp.float32
ANY = pl.BlockSpec(memory_space=pl.ANY)
VMEM = pl.BlockSpec(memory_space=pltpu.VMEM)
SMEM = pl.BlockSpec(memory_space=pltpu.SMEM)
DMA = pltpu.SemaphoreType.DMA


def params(mib):
    return pltpu.CompilerParams(vmem_limit_bytes=mib << 20)


def hermite_table(cells):
    index = np.arange(cells, dtype=np.float32)
    points = ((index - np.float32(cells / 2) + np.float32(0.5)) * np.float32(SPAN / cells)).astype(np.float32)
    before = np.zeros_like(points)
    current = (np.float32(math.pi ** (-0.25)) * np.exp(np.float32(-0.5) * points * points)).astype(np.float32)
    collected = []
    for order in range(ORDERS):
        collected.append(current)
        following = (
            np.float32(math.sqrt(2.0 / (order + 1))) * points * current
            - np.float32(math.sqrt(order / (order + 1.0))) * before
        ).astype(np.float32)
        before, current = (current, following)
    return np.stack(collected, axis=0)


def chirp_halves(cells):
    half = cells // 2
    index = np.arange(half, dtype=np.int64)
    offset = index[:, None] - index[None, :]
    square = offset * offset % (2 * cells)
    phase = square.astype(np.float64) * (math.pi / cells)
    factor = cells ** (-0.5)
    real = (np.cos(phase) * factor).astype(np.float32)
    imag = (np.sin(phase) * factor).astype(np.float32)
    even = offset % 2 == 0
    out = []
    for keep in (even, ~even):
        r = np.where(keep, real, 0.0)
        i = np.where(keep, imag, 0.0)
        out.append((r.astype(jnp.bfloat16), i.astype(jnp.bfloat16)))
    return out


def soften(intersection):
    half = intersection.shape[-1] // 2
    real_part = intersection[..., :half]
    imag_part = intersection[..., half:]
    denom = jnp.sqrt(real_part * real_part + imag_part * imag_part + 1.0)
    return intersection / jnp.concatenate([denom, denom], axis=-1)


def swap_cores(block):
    return lax.ppermute(block, "core", [(0, 1), (1, 0)])


def row_of(modes, columns, core):
    picked = columns[:, :, core].reshape(512, ORDERS)
    lanes = lax.broadcasted_iota(jnp.int32, picked.shape, 1)
    return jnp.sum(jnp.where(lanes == modes[0, 0], picked, 0.0), axis=1, keepdims=True)


def bits_of(spot):
    return (spot & 1) ^ (spot >> 1), spot >> 1


def owner_codes():
    out = []
    for yh in range(2):
        for z in range(4):
            for x in range(4):
                for yl in range(2):
                    (ax, bx), (ay, by), (az, bz) = bits_of(x), bits_of(yh * 2 + yl), bits_of(z)
                    out.append((ax * 4 + ay * 2 + az, bx * 4 + by * 2 + bz))
    return out


CODES = owner_codes()


def place_of(block, core):
    a, b = CODES[block]
    return a * 8 + b + core * (7 * b - 7 * a)


def device_groups():
    def device(a, b, core):
        x, y, z = ((a >> k & 1) ^ (3 * (b >> k & 1)) for k in (2, 1, 0))
        return ((((y >> 1) * 4 + z) * 2 + core) * 4 + x) * 2 + (y & 1)

    over_a = [[[device(a, b, core) for a in range(8)] for b in range(8)] for core in range(2)]
    over_b = [[[device(a, b, core) for b in range(8)] for a in range(8)] for core in range(2)]
    return over_a[0] + over_b[1], over_b[0] + over_a[1]


WIDE, NARROW = device_groups()


def own_kernel(modes, table, columns, back, out, buf, sems):
    core = lax.axis_index("core")
    copies = [
        pltpu.make_async_copy(back.at[k // 4, k % 4, core], buf.at[k], sems.at[k]) for k in range(8)
    ]
    for copy in copies:
        copy.start()
    row_func = row_of(modes, columns, core)
    col_func = table[pl.ds(modes[0, 1], 1), :]
    cells = table.shape[1]
    for k in range(8):
        copies[k].wait()
        for j in range(8):
            block = k * 8 + j
            field = (row_func[block * 8 : block * 8 + 8] * col_func).astype(BF16)
            for plane in range(2):
                span = slice(plane * cells, (plane + 1) * cells)
                out[place_of(block, core), :, span] = buf[k, j * 8 : j * 8 + 8, span] * field


def own_product(modes, table, columns, back):
    width = back.shape[-1]
    return pl.pallas_call(
        own_kernel,
        out_shape=jax.ShapeDtypeStruct((64, 8, width), BF16),
        in_specs=[SMEM, VMEM, VMEM, ANY],
        out_specs=VMEM,
        scratch_shapes=[pltpu.VMEM((8, 64, width), BF16), DMA((8,))],
        compiler_params=params(14),
        cost_estimate=pl.CostEstimate(flops=2 << 20, bytes_accessed=4 << 20, transcendentals=0),
        name="own_product",
    )(modes, table, columns, back)


def both_kernel(peer, table, columns, got, keep, out):
    core = lax.axis_index("core")
    row_func = row_of(peer, columns, core)
    col_func = table[pl.ds(peer[0, 1], 1), :]
    cells = table.shape[1]
    for block in range(64):
        place = place_of(block, core)
        k, j = block // 8, block % 8
        field = (row_func[block * 8 : block * 8 + 8] * col_func).astype(BF16).astype(F32)
        for plane in range(2):
            span = slice(plane * cells, (plane + 1) * cells)
            value = got[k // 4, k % 4, j * 8 : j * 8 + 8, span].astype(F32) * field
            out[place, :, span] = (value + keep[place, :, span].astype(F32)).astype(BF16)


def both_products(peer, table, columns, got, keep):
    return pl.pallas_call(
        both_kernel,
        out_shape=jax.ShapeDtypeStruct(keep.shape, BF16),
        in_specs=[SMEM] + [VMEM] * 4,
        out_specs=VMEM,
        compiler_params=params(14),
        name="both_products",
    )(peer, table, columns, got, keep)


def spread_half(modes, table, columns, mask, even, odd, plus, minus, sums, diffs, core, slot):
    row_func = row_of(modes, columns, core)
    col_func = table[pl.ds(modes[0, 1], 1), :]
    cells = col_func.shape[1]
    half = cells // 2
    for pair in range(32):
        first, second = (mask[place_of(2 * pair + k, core)] for k in range(2))
        both = jnp.concatenate([first, second], axis=0)
        rows = slice(pair * 16, pair * 16 + 16)
        field = (row_func[rows] * col_func).astype(BF16)
        for plane, value in ((0, both[:, :cells] * field), (1, both[:, cells:] * (-field))):
            span = slice(plane * half, (plane + 1) * half)
            plus[rows, span] = value[:, :half] + value[:, half:]
            minus[rows, span] = value[:, :half] - value[:, half:]
    for n in range(4):
        span = slice(n * 256, (n + 1) * 256)
        e = jnp.dot(plus[...], even[:, :, :, :, span].reshape(cells, 256), preferred_element_type=F32)
        o = jnp.dot(minus[...], odd[:, :, :, :, span].reshape(cells, 256), preferred_element_type=F32)
        plane, at = n // 2, (n % 2) * 256
        for shift, value in ((0, e + o), (half, e - o)):
            value = (-value if plane else value).astype(BF16)
            top, bottom = value[:256], value[256:]
            where = slice(at + shift, at + shift + 256)
            sums[plane, :, slot, :, where] = (top + bottom).reshape(4, 64, 256)
            diffs[plane, :, slot, :, where] = (top - bottom).reshape(4, 64, 256)


def second_half(even, odd, sums, diffs, back, out, core, chunks):
    cells = sums.shape[-1]
    wide = out.shape[-1] // 2
    rows_even = even[:, :, core].reshape(512, cells)
    rows_odd = odd[:, :, core].reshape(512, cells)
    for n in chunks:
        span = slice(n * 256, (n + 1) * 256)
        other = slice(cells + n * 256, cells + (n + 1) * 256)
        at = (n - chunks[0]) * 256
        right_even = sums[:, :, :, :, span].reshape(cells, 256)
        right_odd = diffs[:, :, :, :, span].reshape(cells, 256)
        e, o = (
            [jnp.dot(rows[k * 256 : k * 256 + 256], right, preferred_element_type=F32) for k in range(2)]
            for rows, right in ((rows_even, right_even), (rows_odd, right_odd))
        )
        for j in range(32):
            for h in range(2):
                rows = slice(j * 8, j * 8 + 8)
                real = e[0][rows] - o[0][rows] if h else e[0][rows] + o[0][rows]
                imag = e[1][rows] - o[1][rows] if h else e[1][rows] + o[1][rows]
                inner = slice(j % 8 * 8, j % 8 * 8 + 8)
                back_real = back[h, j // 8, core, inner, span].astype(F32)
                back_imag = back[h, j // 8, core, inner, other].astype(F32)
                place = place_of(h * 32 + j, core)
                out[place, :, at : at + 256] = (back_real * real + back_imag * imag).astype(BF16)
                out[place, :, wide + at : wide + at + 256] = (back_imag * real - back_real * imag).astype(BF16)


def spread_kernel(modes, table, columns, mask, even, odd, sums, diffs, plus, minus):
    core = lax.axis_index("core")
    spread_half(modes, table, columns, mask, even, odd, plus, minus, sums, diffs, core, 0)


def spread_own(modes, table, columns, mask, even, odd):
    cells = even.shape[-1]
    shape = jax.ShapeDtypeStruct((2, 4, 1, 64, cells), BF16)
    return pl.pallas_call(
        spread_kernel,
        out_shape=(shape, shape),
        in_specs=[SMEM] + [VMEM] * 5,
        out_specs=(VMEM, VMEM),
        scratch_shapes=[pltpu.VMEM((512, cells), BF16)] * 2,
        compiler_params=params(20),
        name="spread_own",
    )(modes, table, columns, mask, even, odd)


def arrive_kernel(modes, table, columns, mask, even, odd, own_sums, own_diffs, back, out, sums, diffs, plus, minus):
    core = lax.axis_index("core")
    other = 1 - core
    spread_half(modes, table, columns, mask, even, odd, plus, minus, sums, diffs, other, other)
    sums[:, :, core] = own_sums[:, :, 0]
    diffs[:, :, core] = own_diffs[:, :, 0]
    second_half(even, odd, sums, diffs, back, out, other, (0, 1))


def arrive_away(modes, table, columns, mask, even, odd, own_sums, own_diffs, back):
    cells = back.shape[-1] // 2
    shape = jax.ShapeDtypeStruct((2, 4, 2, 64, cells), BF16)
    return pl.pallas_call(
        arrive_kernel,
        out_shape=(jax.ShapeDtypeStruct((64, 8, cells), BF16), shape, shape),
        in_specs=[SMEM] + [VMEM] * 8,
        out_specs=(VMEM, VMEM, VMEM),
        scratch_shapes=[pltpu.VMEM((512, cells), BF16)] * 2,
        compiler_params=params(32),
        name="arrive_away",
    )(modes, table, columns, mask, even, odd, own_sums, own_diffs, back)


def rest_kernel(away, even, odd, sums, diffs, back, out):
    core = lax.axis_index("core")
    if away:
        core = 1 - core
    second_half(even, odd, sums, diffs, back, out, core, (2, 3) if away else (0, 1, 2, 3))


def arrive_rest(away, even, odd, sums, diffs, back):
    width = back.shape[-1]
    return pl.pallas_call(
        functools.partial(rest_kernel, away),
        out_shape=jax.ShapeDtypeStruct((64, 8, width // 2 if away else width), BF16),
        in_specs=[VMEM] * 5,
        out_specs=VMEM,
        compiler_params=params(22),
        cost_estimate=pl.CostEstimate(flops=(2 << 30) >> away, bytes_accessed=8 << 20, transcendentals=0),
        name="arrive_rest" if away else "arrive_keep",
    )(even, odd, sums, diffs, back)


def join_kernel(keep, first, second, out):
    half = first.shape[-1] // 2
    for place in range(64):
        for n in range(4):
            part = (first, second)[n % 2][place, :, (n // 2) * half : (n // 2 + 1) * half]
            span = slice(n * half, (n + 1) * half)
            out[place, :, span] = (keep[place, :, span].astype(F32) + part.astype(F32)).astype(BF16)


def join(keep, first, second):
    return pl.pallas_call(
        join_kernel,
        out_shape=jax.ShapeDtypeStruct(keep.shape, BF16),
        in_specs=[VMEM] * 3,
        out_specs=VMEM,
        compiler_params=params(14),
        name="join",
    )(keep, first, second)


def exchange(blocks, groups):
    return lax.all_to_all(blocks, AXES, 0, 0, tiled=True, axis_index_groups=groups)


def total(parts):
    kept = [parts[k].astype(F32) for k in range(len(parts))]
    while len(kept) > 1:
        kept = [kept[k] + kept[k + 1] for k in range(0, len(kept), 2)]
    return kept[0]


def halve_rows(both):
    width = both.shape[-1]
    return total(exchange(both.reshape(8, 64, width), WIDE)).astype(BF16)


def own_place():
    pairs = [bits_of(lax.axis_index("x")), bits_of(lax.axis_index("yh") * 2 + lax.axis_index("yl"))]
    pairs.append(bits_of(lax.axis_index("z")))
    a, b = (pairs[0][k] * 4 + pairs[1][k] * 2 + pairs[2][k] for k in range(2))
    return b + lax.axis_index("core") * (a - b)


def mask_kernel(scale, near, low, own, every):
    cells = near.shape[-1] // 2
    for block in range(8):
        rows = slice(block * 8, block * 8 + 8)
        real = total([near[k, rows, :cells] for k in range(8)]) * scale
        imag = total([near[k, rows, cells:] for k in range(8)]) * scale
        inverse = 1.0 / jnp.sqrt(real * real + imag * imag + 1.0)
        for span, part in ((slice(0, cells), real), (slice(cells, 2 * cells), imag)):
            part = part * inverse
            every[block, :, span] = part
            part = part.astype(BF16)
            for k in range(8):
                low[k, rows, span] = part
    own[...] = every[own_place()]


def mask_rows(near, scale):
    width = near.shape[-1]
    return pl.pallas_call(
        functools.partial(mask_kernel, scale),
        out_shape=(jax.ShapeDtypeStruct((8, 64, width), BF16), jax.ShapeDtypeStruct((8, width), F32)),
        in_specs=[VMEM],
        out_specs=(VMEM, VMEM),
        scratch_shapes=[pltpu.VMEM((8, 8, width), F32)],
        compiler_params=params(12),
        name="mask_rows",
    )(near)


def body(modes, back_first, back_second):
    cells = back_first.shape[1]
    scale_all = float(128) ** (-0.5)
    host_table = hermite_table(cells)
    table = jnp.asarray(host_table)
    columns = jnp.asarray(host_table.T.copy()).reshape(2, 4, 2, 64, ORDERS)
    (even_r, even_i), (odd_r, odd_i) = jax.tree.map(jnp.asarray, chirp_halves(cells))
    even = jnp.block([[even_r, -even_i], [even_i, even_r]]).reshape(2, 4, 2, 64, cells)
    odd = jnp.block([[odd_r, -odd_i], [odd_i, odd_r]]).reshape(2, 4, 2, 64, cells)
    back_first = back_first.reshape(2, 4, 2, 64, 2 * cells)
    back_second = back_second.reshape(2, 4, 2, 64, 2 * cells)
    peer = swap_cores(modes)
    away = lax.dynamic_index_in_dim(back_first, 1 - lax.axis_index("core"), 2, keepdims=False)
    got = swap_cores(away)
    keep = own_product(modes, table, columns, back_first)
    partial = halve_rows(both_products(peer, table, columns, got, keep))
    width = 2 * cells
    near = exchange(jnp.broadcast_to(partial[None], (8, 64, width)), NARROW)
    low, mask_first = mask_rows(near, scale_all)
    mine = exchange(low, WIDE).reshape(64, 8, width)
    other = swap_cores(mine)
    own = spread_own(modes, table, columns, mine, even, odd)
    away, sums, diffs = arrive_away(modes, table, columns, other, even, odd, *own, back_second)
    first = swap_cores(away)
    second = swap_cores(arrive_rest(True, even, odd, sums, diffs, back_second))
    keep = arrive_rest(False, even, odd, sums, diffs, back_second)
    partial = halve_rows(join(keep, first, second))
    parts = exchange(partial.reshape(8, 8, width), NARROW)
    mask_second = soften(total(parts) * scale_all)
    return (mask_first, mask_second)


def solution(mesh):
    fine = Mesh(mesh.devices.reshape(2, 4, 2, 4, 2), AXES)
    placed = (P(AXES, None), P(AXES, None, None), P(AXES, None, None))
    return jax.shard_map(
        body, mesh=fine, in_specs=placed, out_specs=(P(AXES, None), P(AXES, None)), check_vma=False
    )
```

```python
import functools
import math

import jax
import jax.numpy as jnp
import numpy as np
from jax import lax
from jax.experimental import pallas as pl
from jax.experimental.pallas import tpu as pltpu
from jax.sharding import Mesh
from jax.sharding import PartitionSpec as P

ORDERS = 32
SPAN = 24.0
AXES = ("yh", "z", "core", "x", "yl")
BF16 = jnp.bfloat16
F32 = jnp.float32
ANY = pl.BlockSpec(memory_space=pl.ANY)
VMEM = pl.BlockSpec(memory_space=pltpu.VMEM)
SMEM = pl.BlockSpec(memory_space=pltpu.SMEM)
DMA = pltpu.SemaphoreType.DMA


def params(mib):
    return pltpu.CompilerParams(vmem_limit_bytes=mib << 20)


def hermite_table(cells):
    index = np.arange(cells, dtype=np.float32)
    points = ((index - np.float32(cells / 2) + np.float32(0.5)) * np.float32(SPAN / cells)).astype(np.float32)
    before = np.zeros_like(points)
    current = (np.float32(math.pi ** (-0.25)) * np.exp(np.float32(-0.5) * points * points)).astype(np.float32)
    collected = []
    for order in range(ORDERS):
        collected.append(current)
        following = (
            np.float32(math.sqrt(2.0 / (order + 1))) * points * current
            - np.float32(math.sqrt(order / (order + 1.0))) * before
        ).astype(np.float32)
        before, current = (current, following)
    return np.stack(collected, axis=0)


def chirp_halves(cells):
    half = cells // 2
    index = np.arange(half, dtype=np.int64)
    offset = index[:, None] - index[None, :]
    square = offset * offset % (2 * cells)
    phase = square.astype(np.float64) * (math.pi / cells)
    factor = cells ** (-0.5)
    real = (np.cos(phase) * factor).astype(np.float32)
    imag = (np.sin(phase) * factor).astype(np.float32)
    even = offset % 2 == 0
    out = []
    for keep in (even, ~even):
        r = np.where(keep, real, 0.0)
        i = np.where(keep, imag, 0.0)
        out.append((r.astype(jnp.bfloat16), i.astype(jnp.bfloat16)))
    return out


def soften(intersection):
    half = intersection.shape[-1] // 2
    real_part = intersection[..., :half]
    imag_part = intersection[..., half:]
    denom = jnp.sqrt(real_part * real_part + imag_part * imag_part + 1.0)
    return intersection / jnp.concatenate([denom, denom], axis=-1)


def swap_cores(block):
    return lax.ppermute(block, "core", [(0, 1), (1, 0)])


def row_of(modes, columns, core):
    picked = columns[:, :, core].reshape(512, ORDERS)
    lanes = lax.broadcasted_iota(jnp.int32, picked.shape, 1)
    return jnp.sum(jnp.where(lanes == modes[0, 0], picked, 0.0), axis=1, keepdims=True)


def bits_of(spot):
    return (spot & 1) ^ (spot >> 1), spot >> 1


def owner_codes():
    out = []
    for yh in range(2):
        for z in range(4):
            for x in range(4):
                for yl in range(2):
                    (ax, bx), (ay, by), (az, bz) = bits_of(x), bits_of(yh * 2 + yl), bits_of(z)
                    out.append((ax * 4 + ay * 2 + az, bx * 4 + by * 2 + bz))
    return out


CODES = owner_codes()


def place_of(block, core):
    a, b = CODES[block]
    return a * 8 + b + core * (7 * b - 7 * a)


def device_groups():
    def device(a, b, core):
        x, y, z = ((a >> k & 1) ^ (3 * (b >> k & 1)) for k in (2, 1, 0))
        return ((((y >> 1) * 4 + z) * 2 + core) * 4 + x) * 2 + (y & 1)

    over_a = [[[device(a, b, core) for a in range(8)] for b in range(8)] for core in range(2)]
    over_b = [[[device(a, b, core) for b in range(8)] for a in range(8)] for core in range(2)]
    return over_a[0] + over_b[1], over_b[0] + over_a[1]


WIDE, NARROW = device_groups()


def own_kernel(modes, table, columns, back, out, buf, sems):
    core = lax.axis_index("core")
    copies = [
        pltpu.make_async_copy(back.at[k // 4, k % 4, core], buf.at[k], sems.at[k]) for k in range(8)
    ]
    for copy in copies:
        copy.start()
    row_func = row_of(modes, columns, core)
    col_func = table[pl.ds(modes[0, 1], 1), :]
    cells = table.shape[1]
    for k in range(8):
        copies[k].wait()
        for j in range(8):
            block = k * 8 + j
            field = (row_func[block * 8 : block * 8 + 8] * col_func).astype(BF16)
            for plane in range(2):
                span = slice(plane * cells, (plane + 1) * cells)
                out[place_of(block, core), :, span] = buf[k, j * 8 : j * 8 + 8, span] * field


def own_product(modes, table, columns, back):
    width = back.shape[-1]
    return pl.pallas_call(
        own_kernel,
        out_shape=jax.ShapeDtypeStruct((64, 8, width), BF16),
        in_specs=[SMEM, VMEM, VMEM, ANY],
        out_specs=VMEM,
        scratch_shapes=[pltpu.VMEM((8, 64, width), BF16), DMA((8,))],
        compiler_params=params(14),
        cost_estimate=pl.CostEstimate(flops=2 << 20, bytes_accessed=4 << 20, transcendentals=0),
        name="own_product",
    )(modes, table, columns, back)


def both_kernel(peer, table, columns, got, keep, out):
    core = lax.axis_index("core")
    row_func = row_of(peer, columns, core)
    col_func = table[pl.ds(peer[0, 1], 1), :]
    cells = table.shape[1]
    for block in range(64):
        place = place_of(block, core)
        k, j = block // 8, block % 8
        field = (row_func[block * 8 : block * 8 + 8] * col_func).astype(BF16)
        for plane in range(2):
            span = slice(plane * cells, (plane + 1) * cells)
            out[place, :, span] = got[k // 4, k % 4, j * 8 : j * 8 + 8, span] * field + keep[place, :, span]


def both_products(peer, table, columns, got, keep):
    return pl.pallas_call(
        both_kernel,
        out_shape=jax.ShapeDtypeStruct(keep.shape, BF16),
        in_specs=[SMEM] + [VMEM] * 4,
        out_specs=VMEM,
        compiler_params=params(14),
        name="both_products",
    )(peer, table, columns, got, keep)


def spread_half(modes, table, columns, mask, even, odd, plus, minus, sums, diffs, core, slot):
    row_func = row_of(modes, columns, core)
    col_func = table[pl.ds(modes[0, 1], 1), :]
    cells = col_func.shape[1]
    half = cells // 2
    for pair in range(32):
        first, second = (mask[place_of(2 * pair + k, core)] for k in range(2))
        both = jnp.concatenate([first, second], axis=0)
        rows = slice(pair * 16, pair * 16 + 16)
        field = (row_func[rows] * col_func).astype(BF16)
        for plane, value in ((0, both[:, :cells] * field), (1, both[:, cells:] * (-field))):
            span = slice(plane * half, (plane + 1) * half)
            plus[rows, span] = value[:, :half] + value[:, half:]
            minus[rows, span] = value[:, :half] - value[:, half:]
    for n in range(4):
        span = slice(n * 256, (n + 1) * 256)
        e = jnp.dot(plus[...], even[:, :, :, :, span].reshape(cells, 256), preferred_element_type=F32)
        o = jnp.dot(minus[...], odd[:, :, :, :, span].reshape(cells, 256), preferred_element_type=F32)
        plane, at = n // 2, (n % 2) * 256
        for shift, value in ((0, e + o), (half, e - o)):
            value = (-value if plane else value).astype(BF16)
            top, bottom = value[:256], value[256:]
            where = slice(at + shift, at + shift + 256)
            sums[plane, :, slot, :, where] = (top + bottom).reshape(4, 64, 256)
            diffs[plane, :, slot, :, where] = (top - bottom).reshape(4, 64, 256)


def second_half(even, odd, sums, diffs, back, out, core, chunks):
    cells = sums.shape[-1]
    wide = out.shape[-1] // 2
    rows_even = even[:, :, core].reshape(512, cells)
    rows_odd = odd[:, :, core].reshape(512, cells)
    for n in chunks:
        span = slice(n * 256, (n + 1) * 256)
        other = slice(cells + n * 256, cells + (n + 1) * 256)
        at = (n - chunks[0]) * 256
        right_even = sums[:, :, :, :, span].reshape(cells, 256)
        right_odd = diffs[:, :, :, :, span].reshape(cells, 256)
        e, o = (
            [jnp.dot(rows[k * 256 : k * 256 + 256], right, preferred_element_type=F32) for k in range(2)]
            for rows, right in ((rows_even, right_even), (rows_odd, right_odd))
        )
        for j in range(32):
            for h in range(2):
                rows = slice(j * 8, j * 8 + 8)
                real = e[0][rows] - o[0][rows] if h else e[0][rows] + o[0][rows]
                imag = e[1][rows] - o[1][rows] if h else e[1][rows] + o[1][rows]
                inner = slice(j % 8 * 8, j % 8 * 8 + 8)
                back_real = back[h, j // 8, core, inner, span].astype(F32)
                back_imag = back[h, j // 8, core, inner, other].astype(F32)
                place = place_of(h * 32 + j, core)
                out[place, :, at : at + 256] = (back_real * real + back_imag * imag).astype(BF16)
                out[place, :, wide + at : wide + at + 256] = (back_imag * real - back_real * imag).astype(BF16)


def spread_kernel(modes, table, columns, mask, even, odd, sums, diffs, plus, minus):
    core = lax.axis_index("core")
    spread_half(modes, table, columns, mask, even, odd, plus, minus, sums, diffs, core, 0)


def spread_own(modes, table, columns, mask, even, odd):
    cells = even.shape[-1]
    shape = jax.ShapeDtypeStruct((2, 4, 1, 64, cells), BF16)
    return pl.pallas_call(
        spread_kernel,
        out_shape=(shape, shape),
        in_specs=[SMEM] + [VMEM] * 5,
        out_specs=(VMEM, VMEM),
        scratch_shapes=[pltpu.VMEM((512, cells), BF16)] * 2,
        compiler_params=params(20),
        name="spread_own",
    )(modes, table, columns, mask, even, odd)


def arrive_kernel(modes, table, columns, mask, even, odd, own_sums, own_diffs, back, out, sums, diffs, plus, minus):
    core = lax.axis_index("core")
    other = 1 - core
    spread_half(modes, table, columns, mask, even, odd, plus, minus, sums, diffs, other, other)
    sums[:, :, core] = own_sums[:, :, 0]
    diffs[:, :, core] = own_diffs[:, :, 0]
    second_half(even, odd, sums, diffs, back, out, other, (0, 1))


def arrive_away(modes, table, columns, mask, even, odd, own_sums, own_diffs, back):
    cells = back.shape[-1] // 2
    shape = jax.ShapeDtypeStruct((2, 4, 2, 64, cells), BF16)
    return pl.pallas_call(
        arrive_kernel,
        out_shape=(jax.ShapeDtypeStruct((64, 8, cells), BF16), shape, shape),
        in_specs=[SMEM] + [VMEM] * 8,
        out_specs=(VMEM, VMEM, VMEM),
        scratch_shapes=[pltpu.VMEM((512, cells), BF16)] * 2,
        compiler_params=params(32),
        name="arrive_away",
    )(modes, table, columns, mask, even, odd, own_sums, own_diffs, back)


def rest_kernel(away, even, odd, sums, diffs, back, out):
    core = lax.axis_index("core")
    if away:
        core = 1 - core
    second_half(even, odd, sums, diffs, back, out, core, (2, 3) if away else (0, 1, 2, 3))


def arrive_rest(away, even, odd, sums, diffs, back):
    width = back.shape[-1]
    return pl.pallas_call(
        functools.partial(rest_kernel, away),
        out_shape=jax.ShapeDtypeStruct((64, 8, width // 2 if away else width), BF16),
        in_specs=[VMEM] * 5,
        out_specs=VMEM,
        compiler_params=params(22),
        cost_estimate=pl.CostEstimate(flops=(2 << 30) >> away, bytes_accessed=8 << 20, transcendentals=0),
        name="arrive_rest" if away else "arrive_keep",
    )(even, odd, sums, diffs, back)


def join_kernel(keep, first, second, out):
    half = first.shape[-1] // 2
    for place in range(64):
        for n in range(4):
            part = (first, second)[n % 2][place, :, (n // 2) * half : (n // 2 + 1) * half]
            span = slice(n * half, (n + 1) * half)
            out[place, :, span] = keep[place, :, span] + part


def join(keep, first, second):
    return pl.pallas_call(
        join_kernel,
        out_shape=jax.ShapeDtypeStruct(keep.shape, BF16),
        in_specs=[VMEM] * 3,
        out_specs=VMEM,
        compiler_params=params(14),
        name="join",
    )(keep, first, second)


def exchange(blocks, groups):
    return lax.all_to_all(blocks, AXES, 0, 0, tiled=True, axis_index_groups=groups)


def total(parts):
    kept = [parts[k].astype(F32) for k in range(len(parts))]
    while len(kept) > 1:
        kept = [kept[k] + kept[k + 1] for k in range(0, len(kept), 2)]
    return kept[0]


def halve_rows(both):
    width = both.shape[-1]
    return total(exchange(both.reshape(8, 64, width), WIDE)).astype(BF16)


def partial_kernel(wide, out):
    half = wide.shape[-1] // 2
    for block in range(8):
        rows = slice(block * 8, block * 8 + 8)
        for span in (slice(0, half), slice(half, 2 * half)):
            part = total([wide[k, rows, span] for k in range(8)]).astype(BF16)
            for k in range(8):
                out[k, rows, span] = part


def partial_rows(wide):
    return pl.pallas_call(
        partial_kernel,
        out_shape=jax.ShapeDtypeStruct(wide.shape, BF16),
        in_specs=[VMEM],
        out_specs=VMEM,
        compiler_params=params(12),
        name="partial_rows",
    )(wide)


def own_place():
    pairs = [bits_of(lax.axis_index("x")), bits_of(lax.axis_index("yh") * 2 + lax.axis_index("yl"))]
    pairs.append(bits_of(lax.axis_index("z")))
    a, b = (pairs[0][k] * 4 + pairs[1][k] * 2 + pairs[2][k] for k in range(2))
    return b + lax.axis_index("core") * (a - b)


def mask_kernel(scale, near, low, own, every):
    cells = near.shape[-1] // 2
    for block in range(8):
        rows = slice(block * 8, block * 8 + 8)
        real = total([near[k, rows, :cells] for k in range(8)]) * scale
        imag = total([near[k, rows, cells:] for k in range(8)]) * scale
        inverse = 1.0 / jnp.sqrt(real * real + imag * imag + 1.0)
        for span, part in ((slice(0, cells), real), (slice(cells, 2 * cells), imag)):
            part = part * inverse
            every[block, :, span] = part
            part = part.astype(BF16)
            for k in range(8):
                low[k, rows, span] = part
    own[...] = every[own_place()]


def mask_rows(near, scale):
    width = near.shape[-1]
    return pl.pallas_call(
        functools.partial(mask_kernel, scale),
        out_shape=(jax.ShapeDtypeStruct((8, 64, width), BF16), jax.ShapeDtypeStruct((8, width), F32)),
        in_specs=[VMEM],
        out_specs=(VMEM, VMEM),
        scratch_shapes=[pltpu.VMEM((8, 8, width), F32)],
        compiler_params=params(12),
        name="mask_rows",
    )(near)


def body(modes, back_first, back_second):
    cells = back_first.shape[1]
    scale_all = float(128) ** (-0.5)
    host_table = hermite_table(cells)
    table = jnp.asarray(host_table)
    columns = jnp.asarray(host_table.T.copy()).reshape(2, 4, 2, 64, ORDERS)
    (even_r, even_i), (odd_r, odd_i) = jax.tree.map(jnp.asarray, chirp_halves(cells))
    even = jnp.block([[even_r, -even_i], [even_i, even_r]]).reshape(2, 4, 2, 64, cells)
    odd = jnp.block([[odd_r, -odd_i], [odd_i, odd_r]]).reshape(2, 4, 2, 64, cells)
    back_first = back_first.reshape(2, 4, 2, 64, 2 * cells)
    back_second = back_second.reshape(2, 4, 2, 64, 2 * cells)
    peer = swap_cores(modes)
    away = lax.dynamic_index_in_dim(back_first, 1 - lax.axis_index("core"), 2, keepdims=False)
    got = swap_cores(away)
    keep = own_product(modes, table, columns, back_first)
    width = 2 * cells
    both = both_products(peer, table, columns, got, keep)
    near = exchange(partial_rows(exchange(both.reshape(8, 64, width), WIDE)), NARROW)
    low, mask_first = mask_rows(near, scale_all)
    mine = exchange(low, WIDE).reshape(64, 8, width)
    other = swap_cores(mine)
    own = spread_own(modes, table, columns, mine, even, odd)
    away, sums, diffs = arrive_away(modes, table, columns, other, even, odd, *own, back_second)
    first = swap_cores(away)
    rest = arrive_rest(True, even, odd, sums, diffs, back_second)
    second = swap_cores(rest)
    keep = arrive_rest(False, even, odd, sums, diffs, back_second)
    partial = halve_rows(join(keep, first, second))
    parts = exchange(partial.reshape(8, 8, width), NARROW)
    mask_second = soften(total(parts) * scale_all)
    return (mask_first, mask_second)


def solution(mesh):
    fine = Mesh(mesh.devices.reshape(2, 4, 2, 4, 2), AXES)
    placed = (P(AXES, None), P(AXES, None, None), P(AXES, None, None))
    return jax.shard_map(
        body, mesh=fine, in_specs=placed, out_specs=(P(AXES, None), P(AXES, None)), check_vma=False
    )
```
